32 devices in a mesh: dev: 32 (over z, y, x, core).
Axes of the slice: x: 2, y: 2, z: 4, core: 2. Of those that a mesh axis runs over, the one named last changes fastest.
Arguments:
- density_rows: bfloat16 [24576, 3840], P('dev')
- center_x: float32 [24576], replicated, may hold values from -0.25 to 1.25
- center_y: float32 [24576], replicated, may hold values from 0 to 1
- center_z: float32 [24576], replicated, may hold values from 0 to 1
- exponent: float32 [24576], replicated, may hold values from 0.5 to 150
- brick_blocks: int32 [32, 8], replicated, may hold values from 0 to 191, as said below
Outputs:
- potential: float32 [32, 4096], P('dev')
- ham_rows: float32 [24576, 3840], P('dev')
The draws below stay inside these ranges and needn't reach their ends.
Inputs may be any that keep to these rules, and one draw needn't show every extreme that they name: `brick_blocks`: brick b belongs to device d = b. Its 8 entries are distinct blocks; 4 of them are owned by one of the devices d - 1, d, d + 1 (cyclically) and 2 by each of the other two, where block I is owned by device I // 6. Which of the three owns 4 changes from brick to brick. Blocks 0 and 191 touch brick 0.
All inputs are finite; a program needn't handle non-finite values.
Results may differ from the reference program's by a relative error of at most 0.00041.
Values may be sent and summed in bfloat16 or wider, within the bound.
A program may use at most 128 MiB of HBM per device.

```python
import math
import jax
import jax.numpy as jnp
from jax import lax

FB = 128
KB = 8
CAP = 4
BLK_DEV = 6
SIDE = 16
BR_DEV = 1
NF = 24576
N_DEV = 32


def draw_density_rows(key, part):
    row_count = N_DEV * BLK_DEV * FB
    col_count = 5 * BLK_DEV * FB
    row_index = jnp.arange(row_count, dtype=jnp.int32)[:, None]
    col_index = jnp.arange(col_count, dtype=jnp.int32)[None, :]
    owner_dev = (row_index // (BLK_DEV * FB)).astype(jnp.float32)
    growth = 1.0 + 2.0 * owner_dev / (N_DEV - 1)
    on_diagonal = col_index == 2 * BLK_DEV * FB + row_index % (BLK_DEV * FB)
    random_part = jnp.clip(jax.random.normal(key, (row_count, col_count), jnp.float32), -6.0, 6.0)
    values = (0.2 * random_part + 2.0 * growth * on_diagonal.astype(jnp.float32)) / (KB * FB)
    return values.astype(jnp.bfloat16)


def draw_brick_blocks(key, part):
    base_key = jax.random.fold_in(key, 11)

    def one_brick(brick):
        brick_key = jax.random.fold_in(base_key, brick)
        device = brick // BR_DEV
        heavy_side = jax.random.randint(jax.random.fold_in(brick_key, 7), (), 0, 3)
        counts = jnp.where(jnp.arange(3) == heavy_side, CAP, (KB - CAP) // 2)
        owners = jnp.mod(device + jnp.arange(3) - 1, N_DEV)
        shuffled_list = []
        for side in range(3):
            perm = jax.random.permutation(jax.random.fold_in(brick_key, side), BLK_DEV).astype(jnp.int32)
            target = jnp.where(owners[side] == 0, 0, jnp.where(owners[side] == N_DEV - 1, BLK_DEV - 1, -1))
            found = (perm == target).astype(jnp.int32)
            position = jnp.sum(found * jnp.arange(BLK_DEV, dtype=jnp.int32))
            rolled = perm[jnp.mod(jnp.arange(BLK_DEV, dtype=jnp.int32) + position, BLK_DEV)]
            use_roll = (brick == 0) & (target >= 0)
            shuffled_list.append(jnp.where(use_roll, rolled, perm))
        shuffled = jnp.stack(shuffled_list)
        chosen = jnp.arange(BLK_DEV)[None, :] < counts[:, None]
        ordering = jnp.argsort(jnp.where(chosen, 0, 1).reshape(-1), stable=True)[:KB]
        blocks = (owners[:, None] * BLK_DEV + shuffled).reshape(-1)
        return blocks[ordering].astype(jnp.int32)
    return lax.map(one_brick, jnp.arange(N_DEV * BR_DEV, dtype=jnp.int32))


def setup_inputs(seed: int = 0) -> dict:
    key_of = jax.random.split(jax.random.key(seed), 7)
    return {
        "density_rows": draw_density_rows(jax.random.fold_in(key_of[6], 71), 0),
        "center_x": jnp.clip(jax.random.uniform(key_of[1], (NF,), jnp.float32, -0.25, 1.25), -0.25, 1.25),
        "center_y": jnp.clip(jax.random.uniform(key_of[2], (NF,), jnp.float32, 0.0, 1.0), 0.0, 1.0),
        "center_z": jnp.clip(jax.random.uniform(key_of[3], (NF,), jnp.float32, 0.0, 1.0), 0.0, 1.0),
        "exponent": jnp.clip(jnp.exp(jax.random.uniform(key_of[4], (NF,), jnp.float32, math.log(0.5), math.log(150.0))), 0.5, 150.0),
        "brick_blocks": draw_brick_blocks(jax.random.fold_in(key_of[6], 71), 0),
    }


omega = 2.0 / 3.0
four_pi = 4.0 * math.pi
slater = (3.0 / math.pi) ** (1.0 / 3.0)


def periodic(distance, period):
    return jnp.mod(distance + 0.5 * period, period) - 0.5 * period


def basis_values(device, z_slot, blocks, center_x, center_y, center_z, exponent, devices):
    functions = (blocks[:, None] * FB + jnp.arange(FB, dtype=jnp.int32)[None, :]).reshape(-1)
    owner_dev = functions // (BLK_DEV * FB)
    offset = (jnp.mod(device - owner_dev + 1, devices) - 1).astype(jnp.float32)
    grid_points = (jnp.arange(SIDE, dtype=jnp.float32) + 0.5) / SIDE
    decay_rate = exponent[functions][:, None]
    along_x = offset[:, None] + grid_points[None, :] - center_x[functions][:, None]
    along_y = periodic(grid_points[None, :] - center_y[functions][:, None], 1.0)
    along_z = periodic(z_slot + grid_points[None, :] - center_z[functions][:, None], 1.0 * BR_DEV)
    factor_x = jnp.exp(-decay_rate * along_x * along_x)
    factor_y = jnp.exp(-decay_rate * along_y * along_y)
    factor_z = jnp.exp(-decay_rate * along_z * along_z)
    values = factor_x[:, :, None, None] * factor_y[:, None, :, None] * factor_z[:, None, None, :]
    return values.reshape(functions.shape[0], SIDE * SIDE * SIDE).astype(jnp.bfloat16)


def reference(density_rows, center_x, center_y, center_z, exponent, brick_blocks):
    nbricks = N_DEV * BR_DEV
    cells = SIDE * SIDE * SIDE
    density_tiles = density_rows.reshape(N_DEV * BLK_DEV, FB, 5 * BLK_DEV, FB)

    def layout(brick):
        blocks = brick_blocks[brick]
        owner_dev = blocks // BLK_DEV
        col_blocks = jnp.mod(owner_dev[None, :] - owner_dev[:, None] + 2, N_DEV) * BLK_DEV + (blocks % BLK_DEV)[None, :]
        orbitals = basis_values((brick // BR_DEV).astype(jnp.int32), (brick % BR_DEV).astype(jnp.float32), blocks,
                                center_x, center_y, center_z, exponent, N_DEV)
        return blocks, col_blocks, orbitals

    def one_density(brick):
        blocks, col_blocks, orbitals = layout(brick)
        pieces = density_tiles[blocks[:, None], :, col_blocks, :]
        matrix = pieces.transpose(0, 2, 1, 3).reshape(KB * FB, KB * FB)
        applied = jnp.dot(matrix, orbitals, preferred_element_type=jnp.float32)
        return jnp.sum(orbitals.astype(jnp.float32) * applied, axis=0)

    density = lax.map(one_density, jnp.arange(nbricks, dtype=jnp.int32))
    average = jnp.sum(density) / (nbricks * cells)
    source = density - average
    sweep_one = (omega * four_pi / 6.0) * source
    grid_field = sweep_one.reshape(N_DEV, BR_DEV, SIDE, SIDE, SIDE).transpose(0, 2, 3, 1, 4)
    grid_field = grid_field.reshape(N_DEV * SIDE, SIDE, BR_DEV * SIDE)
    beside_all = jnp.roll(grid_field, 1, 0) + jnp.roll(grid_field, -1, 0)
    beside_all = beside_all + jnp.roll(grid_field, 1, 1) + jnp.roll(grid_field, -1, 1)
    beside_all = beside_all + jnp.roll(grid_field, 1, 2) + jnp.roll(grid_field, -1, 2)
    beside_all = beside_all.reshape(N_DEV, SIDE, SIDE, BR_DEV, SIDE).transpose(0, 3, 1, 2, 4).reshape(nbricks, cells)
    sweep_two = sweep_one + omega * ((four_pi * source + beside_all) / 6.0 - sweep_one)
    potential = sweep_two - slater * jnp.cbrt(density)

    def add_brick(ham_tiles, brick):
        blocks, col_blocks, orbitals = layout(brick)
        weighted = (orbitals.astype(jnp.float32) * potential[brick][None, :]).astype(jnp.bfloat16)
        ham_brick = jnp.dot(weighted, orbitals.T, preferred_element_type=jnp.float32) * (64.0 / cells)
        pieces = ham_brick.reshape(KB, FB, KB, FB).transpose(0, 2, 1, 3)
        return ham_tiles.at[blocks[:, None], :, col_blocks, :].add(pieces), None

    start = jnp.zeros((N_DEV * BLK_DEV, FB, 5 * BLK_DEV, FB), jnp.float32)
    ham_tiles, ignored = lax.scan(add_brick, start, jnp.arange(nbricks, dtype=jnp.int32))
    return potential, ham_tiles.reshape(N_DEV * BLK_DEV * FB, 5 * BLK_DEV * FB)
```

```python
import functools
import math

import jax
import jax.numpy as jnp
from jax import lax
from jax.experimental import pallas as pl
from jax.experimental.pallas import tpu as pltpu
from jax.sharding import PartitionSpec as P

FB = 128
KB = 8
CAP = 4
BLK_DEV = 6
SIDE = 16
LAYER = SIDE * SIDE
CELLS = SIDE * SIDE * SIDE
COLS = 5 * BLK_DEV * FB
ROWS = BLK_DEV * FB
PAIR = 2 * FB
NEAR = 4
BOTH = 6
CHUNK = 4 * LAYER
VMEM_BYTES = 60 * 1024 * 1024

omega = 2.0 / 3.0
four_pi = 4.0 * math.pi
slater = (3.0 / math.pi) ** (1.0 / 3.0)
f32 = jnp.float32
bf16 = jnp.bfloat16


def wrapped(distance):
    moved = distance + 0.5
    return (moved - jnp.floor(moved)) - 0.5


def order_blocks(brick, first, second, bb_ref):
    blocks = [bb_ref[j, brick] for j in range(KB)]
    owners = [block // BLK_DEV for block in blocks]
    keys = [
        jnp.where(owner == first, 0, jnp.where(owner == second, KB, 2 * KB)) + j for j, owner in enumerate(owners)
    ]
    places = [sum((other < key).astype(jnp.int32) for other in keys if other is not key) for key in keys]
    return [
        sum(jnp.where(place == s, block, 0) for place, block in zip(places, blocks)) for s in range(KB)
    ]


def column_block(block, me, devices):
    owner = block // BLK_DEV
    step = jnp.minimum(lax.rem(owner - me + 2 + devices, devices), 4)
    return step * BLK_DEV + lax.rem(block, BLK_DEV)


def pair_of(me):
    return me + 1 - 2 * lax.rem(me, 2)


def across_of(me, devices):
    return lax.rem(me + 2 * lax.rem(me, 2) - 1 + devices, devices)


def factors(block, brick, devices, param_refs):
    point = (lax.broadcasted_iota(jnp.int32, (SIDE, FB), 0).astype(f32) + 0.5) / SIDE
    owner = block // BLK_DEV
    offset = (lax.rem(brick - owner + 1 + devices, devices) - 1).astype(f32)
    mid_x, mid_y, mid_z, rate = [ref[block] for ref in param_refs]
    rate = -rate
    along_x = (offset + point) - mid_x
    along_y = wrapped(point - mid_y)
    along_z = wrapped(point - mid_z)
    return jnp.exp(rate * along_x * along_x), jnp.exp(rate * along_y * along_y), jnp.exp(rate * along_z * along_z)


def plane(factor_y, factor_z, rows_ref):
    for j in range(SIDE):
        rows_ref[j * SIDE : (j + 1) * SIDE, :] = factor_y[j : j + 1] * factor_z
    return rows_ref[...].T


def spread_matrix(spread_ref):
    shape = spread_ref.shape
    source = lax.rem(lax.broadcasted_iota(jnp.int32, shape, 0), SIDE)
    target = lax.broadcasted_iota(jnp.int32, shape, 1) // FB
    spread_ref[...] = jnp.where(source == target, 1.0, 0.0).astype(bf16)


def fill_block(which, a, brick, devices, slot_ref, param_refs, rows_ref, spread_ref, orb_ref):
    factor_x, factor_y, factor_z = factors(slot_ref[which, a], brick, devices, param_refs)
    high = factor_x.astype(bf16)
    rest = factor_x - high.astype(f32)
    middle = rest.astype(bf16)
    low = (rest - middle.astype(f32)).astype(bf16)
    parts = jnp.concatenate([high, middle, low], axis=0)
    factor_yz = plane(factor_y, factor_z, rows_ref)
    start = pl.multiple_of(a * FB, FB)
    for n in range(SIDE // 2):
        wide = lax.dot_general(
            parts,
            spread_ref[:, n * PAIR : (n + 1) * PAIR],
            (((0,), (0,)), ((), ())),
            preferred_element_type=f32,
        )
        for h in range(2):
            one = wide[:, h * FB : (h + 1) * FB]
            i = 2 * n + h
            orb_ref[pl.ds(start, FB), i * LAYER : (i + 1) * LAYER] = jnp.concatenate(
                [one * factor_yz[:, :FB], one * factor_yz[:, FB:]], axis=1
            ).astype(bf16)


def fold(mat_ref, pairs):
    for i in range(pairs):
        for j in range(i + 1, pairs):
            above = mat_ref[i * PAIR : (i + 1) * PAIR, j * PAIR : (j + 1) * PAIR].astype(f32)
            below = mat_ref[j * PAIR : (j + 1) * PAIR, i * PAIR : (i + 1) * PAIR].astype(f32)
            mat_ref[i * PAIR : (i + 1) * PAIR, j * PAIR : (j + 1) * PAIR] = (above + below.T).astype(bf16)


def density_chunk(j, pairs, mat_ref, orb_ref, pd_ref, t):
    cells = pl.ds(pl.multiple_of(j * CHUNK, CHUNK), CHUNK)
    total = jnp.zeros((1, CHUNK), f32)
    for i in range(pairs):
        applied = jnp.dot(
            mat_ref[i * PAIR : (i + 1) * PAIR, i * PAIR :], orb_ref[i * PAIR :, cells], preferred_element_type=f32
        )
        own = orb_ref[i * PAIR : (i + 1) * PAIR, cells].astype(f32)
        total = total + jnp.sum(own * applied, axis=0, keepdims=True)
    for q in range(CHUNK // LAYER):
        pd_ref[t, pl.ds(j * (CHUNK // LAYER) + q, 1), :] = total[:, q * LAYER : (q + 1) * LAYER]


def weigh_block(k, orb_ref, pot_ref, t, wei_ref):
    rows = pl.ds(pl.multiple_of(k * FB, FB), FB)
    for i in range(SIDE):
        cells = slice(i * LAYER, (i + 1) * LAYER)
        level = pot_ref[t, i : i + 1, :] * (64.0 / CELLS)
        wei_ref[rows, cells] = (orb_ref[rows, cells].astype(f32) * level).astype(bf16)


def ham_column(j, pairs, wei_ref, orb_ref, tile_ref):
    rows = PAIR * min(j + 1, pairs)
    here = slice(j * PAIR, (j + 1) * PAIR)
    tile = lax.dot_general(
        wei_ref[0:rows, :], orb_ref[here, :], (((1,), (1,)), ((), ())), preferred_element_type=f32
    )
    tile_ref[0:rows, here] = tile
    if j < pairs:
        for i in range(j):
            tile_ref[here, i * PAIR : (i + 1) * PAIR] = tile[i * PAIR : (i + 1) * PAIR].T


def potential_of(density, before, after, average):
    scale = omega * four_pi / 6.0
    lane = lax.broadcasted_iota(jnp.int32, (SIDE, LAYER), 1) % SIDE
    row = lax.broadcasted_iota(jnp.int32, (SIDE, LAYER), 0)

    def moved(x, steps, axis):
        return pltpu.roll(x, steps % x.shape[axis], axis)

    source = density - average
    one = scale * source
    up = jnp.where(row == 0, scale * (before - average), moved(one, 1, 0))
    down = jnp.where(row == SIDE - 1, scale * (after - average), moved(one, -1, 0))
    beside = up + down + moved(one, SIDE, 1) + moved(one, -SIDE, 1)
    beside = beside + jnp.where(lane == 0, moved(one, 1 - SIDE, 1), moved(one, 1, 1))
    beside = beside + jnp.where(lane == SIDE - 1, moved(one, SIDE - 1, 1), moved(one, -1, 1))
    two = one + omega * ((four_pi * source + beside) / 6.0 - one)
    size = jnp.abs(density)
    safe = jnp.where(size > 0.0, size, 1.0)
    root = jnp.exp(jnp.log(safe) / 3.0)
    root = root - (root - safe / (root * root)) / 3.0
    root = jnp.where(size > 0.0, root, 0.0)
    root = jnp.where(density < 0.0, -root, root)
    return two - slater * root


def main_kernel(
    devices,
    bb_ref,
    rows_hbm,
    cx,
    cy,
    cz,
    ex,
    out_ref,
    tiles_hbm,
    rows_vmem,
    orb_a,
    orb_b,
    mat_a,
    mat_b,
    mat_in,
    mat_out,
    wei_a,
    wei_b,
    tile_a,
    tile_b,
    plane_ref,
    spread_ref,
    pd_ref,
    pot_ref,
    sum_ref,
    full_in,
    before_in,
    after_in,
    sums,
    slot_ref,
    col_ref,
    load_sem,
    mat_sem,
    send_sem,
    recv_sem,
    all_sem,
    tile_sem,
    tile_send,
    tile_recv,
):
    me = lax.axis_index("dev")
    odd = lax.rem(me, 2)
    pair = pair_of(me)
    across = across_of(me, devices)
    barrier = pltpu.get_barrier_semaphore()

    def at(step):
        return lax.rem(me + step + devices, devices)

    def greet(k, carry):
        pl.semaphore_signal(barrier, inc=1, device_id=(at(k),), device_id_type=pl.DeviceIdType.MESH)
        return carry

    def load(c, carry):
        col = pl.ds(pl.multiple_of(c * FB, FB), FB)
        pltpu.make_async_copy(rows_hbm.at[:, :, col], rows_vmem.at[:, c], load_sem).start()
        return carry

    lax.fori_loop(0, 5 * BLK_DEV, load, 0)
    lax.fori_loop(1, devices, greet, 0)

    lists = ((across, me, me), (me, pair, me), (pair, me, pair))
    for which, (brick, first, second) in enumerate(lists):
        for s, block in enumerate(order_blocks(brick, first, second, bb_ref)):
            slot_ref[which, s] = block
            col_ref[which, s] = column_block(block, me, devices)

    params = (cx, cy, cz, ex)
    spread_matrix(spread_ref)

    def fill_a(a, carry):
        fill_block(0, a, across, devices, slot_ref, params, plane_ref, spread_ref, orb_a)
        return carry

    def fill_b(a, carry):
        fill_block(1, a, me, devices, slot_ref, params, plane_ref, spread_ref, orb_b)
        return carry

    lax.fori_loop(0, KB, fill_a, 0)
    pltpu.make_async_copy(rows_vmem, rows_vmem, load_sem).wait()

    def gather(which, a, target, other=None):
        block = slot_ref[which, a]
        mine = (block // BLK_DEV == me).astype(f32)
        mask = jnp.full((FB, FB), mine, f32).astype(bf16)
        row = lax.rem(block, BLK_DEV)
        here = slice(a * FB, (a + 1) * FB)
        for c in range(KB):
            there = slice(c * FB, (c + 1) * FB)
            tile = rows_vmem[row, col_ref[which, c]] * mask
            target[here, there] = tile if other is None else tile + other[here, there]

    for a in range(NEAR):
        gather(2, a, mat_out)
    pl.semaphore_wait(barrier, devices - 1)
    for a in range(NEAR):
        gather(0, a, mat_a)
    give = pltpu.make_async_remote_copy(
        src_ref=mat_out,
        dst_ref=mat_in,
        send_sem=mat_sem.at[0],
        recv_sem=mat_sem.at[1],
        device_id=(pair,),
        device_id_type=pl.DeviceIdType.MESH,
    )
    give.start()
    fold(mat_a, 2)
    lax.fori_loop(0, KB, fill_b, 0)

    def density_a(j, carry):
        density_chunk(j, 2, mat_a, orb_a, pd_ref, odd)
        return carry

    def density_b(j, carry):
        density_chunk(j, 3, mat_b, orb_b, pd_ref, 1 - odd)
        return carry

    lax.fori_loop(0, CELLS // CHUNK, density_a, 0)
    give.wait()
    mat_b[0:PAIR, :] = mat_in[0:PAIR, :]
    for a in range(2, NEAR):
        gather(1, a, mat_b, mat_in)
    for a in range(NEAR, BOTH):
        gather(1, a, mat_b)
    fold(mat_b, 3)
    lax.fori_loop(0, CELLS // CHUNK, density_b, 0)
    layer = jnp.sum(pd_ref[0] + pd_ref[1], axis=0, keepdims=True)
    sum_ref[0] = layer[:, :FB] + layer[:, FB:]

    def to_all(k):
        return pltpu.make_async_remote_copy(
            src_ref=sum_ref.at[0],
            dst_ref=sums.at[k - 1],
            send_sem=all_sem.at[0],
            recv_sem=all_sem.at[1],
            device_id=(at(k),),
            device_id_type=pl.DeviceIdType.MESH,
        )

    def start_sum(k, carry):
        to_all(k).start()
        return carry

    low = lax.rem(me - 1 + odd + devices, devices)
    plan = (
        (pd_ref, full_in, across, 0),
        (pd_ref.at[1, pl.ds(8, 8)], before_in.at[odd], lax.rem(low + 2, devices), 1 + odd),
        (pd_ref.at[1, pl.ds(8, 8)], before_in.at[odd], lax.rem(low + 3, devices), 1 + odd),
        (pd_ref.at[0, pl.ds(0, 8)], after_in.at[odd], lax.rem(low - 2 + devices, devices), 3 + odd),
        (pd_ref.at[0, pl.ds(0, 8)], after_in.at[odd], lax.rem(low - 1 + devices, devices), 3 + odd),
    )
    copies = [
        pltpu.make_async_remote_copy(
            src_ref=src,
            dst_ref=dst,
            send_sem=send_sem.at[q],
            recv_sem=recv_sem.at[r],
            device_id=(device,),
            device_id_type=pl.DeviceIdType.MESH,
        )
        for q, (src, dst, device, r) in enumerate(plan)
    ]
    lax.fori_loop(1, devices, start_sum, 0)
    for copy in copies:
        copy.start()
    pltpu.make_async_copy(full_in, full_in, recv_sem.at[0]).wait()
    for s in range(2):
        pltpu.make_async_copy(before_in.at[s], before_in.at[s], recv_sem.at[1 + s]).wait()
        pltpu.make_async_copy(after_in.at[s], after_in.at[s], recv_sem.at[3 + s]).wait()
    pltpu.make_async_copy(sums, sums, all_sem.at[1]).wait()

    total = jnp.sum(sums[...], axis=0) + sum_ref[0]
    average = jnp.sum(total, axis=1, keepdims=True) / (devices * CELLS)
    first = pd_ref[0] + full_in[0]
    second = pd_ref[1] + full_in[1]
    behind = (before_in[0] + before_in[1])[7:]
    ahead = (after_in[0] + after_in[1])[:1]
    pot_ref[0] = potential_of(first, behind, second[:1], average)
    pot_ref[1] = potential_of(second, first[SIDE - 1 :], ahead, average)
    out_ref[...] = pot_ref[1 - odd]

    def weigh_a(k, carry):
        weigh_block(k, orb_a, pot_ref, odd, wei_a)
        return carry

    def weigh_b(k, carry):
        weigh_block(k, orb_b, pot_ref, 1 - odd, wei_b)
        return carry

    lax.fori_loop(0, BOTH, weigh_b, 0)

    def give_tiles(n, cells):
        return pltpu.make_async_remote_copy(
            src_ref=tile_b.at[pl.ds(0, NEAR * FB), cells],
            dst_ref=tiles_hbm.at[2, :, cells],
            send_sem=tile_send.at[n],
            recv_sem=tile_recv.at[n],
            device_id=(pair,),
            device_id_type=pl.DeviceIdType.MESH,
        )

    gives = [give_tiles(0, pl.ds(0, 2 * PAIR)), give_tiles(1, pl.ds(2 * PAIR, PAIR)), give_tiles(2, pl.ds(3 * PAIR, PAIR))]
    ham_column(0, 3, wei_b, orb_b, tile_b)
    ham_column(1, 3, wei_b, orb_b, tile_b)
    gives[0].start()
    ham_column(2, 3, wei_b, orb_b, tile_b)
    gives[1].start()
    ham_column(3, 3, wei_b, orb_b, tile_b)
    gives[2].start()
    keep_b = pltpu.make_async_copy(tile_b.at[pl.ds(PAIR, NEAR * FB)], tiles_hbm.at[1], tile_sem.at[1])
    keep_b.start()
    lax.fori_loop(0, NEAR, weigh_a, 0)
    for j in range(4):
        ham_column(j, 2, wei_a, orb_a, tile_a)
    keep_a = pltpu.make_async_copy(tile_a, tiles_hbm.at[0], tile_sem.at[0])
    keep_a.start()
    for copy in copies:
        copy.wait_send()
    pltpu.make_async_copy(sums, sums, all_sem.at[0]).wait()
    for copy in gives:
        copy.wait()
    keep_b.wait()
    keep_a.wait()


def out_kernel(devices, bb_ref, pot_in, tiles_hbm, pot_out, ham_hbm, acc_ref, tiles, slot_ref, col_ref, in_sem, out_sem):
    me = lax.axis_index("dev")
    pair = pair_of(me)
    across = across_of(me, devices)
    lists = ((across, me, me), (me, pair, me), (pair, me, pair))
    first_slot = (0, 2, 0)
    for which, (brick, first, second) in enumerate(lists):
        for s, block in enumerate(order_blocks(brick, first, second, bb_ref)):
            slot_ref[which, s] = block
            col_ref[which, s] = column_block(block, me, devices)

    def place(which, r):
        return sum(
            jnp.where(slot_ref[which, first_slot[which] + s] == me * BLK_DEV + r, s + 1, 0) for s in range(CAP)
        )

    def fetch(which, s):
        rows = pl.ds(pl.multiple_of(s * FB, FB), FB)
        return pltpu.make_async_copy(tiles_hbm.at[which, rows], tiles.at[which, rows], in_sem.at[which, s])

    places = [[place(which, r) for which in range(3)] for r in range(BLK_DEV)]
    for r in range(BLK_DEV):
        for which in range(3):

            @pl.when(places[r][which] > 0)
            def _():
                fetch(which, places[r][which] - 1).start()

    for i in range(SIDE):
        pot_out[:, i * LAYER : (i + 1) * LAYER] = pot_in[i : i + 1, :]
    stores = []
    for r in range(BLK_DEV):
        here = slice(r * FB, (r + 1) * FB)
        acc_ref[here, :] = jnp.zeros((FB, COLS), f32)
        for which in range(3):

            @pl.when(places[r][which] > 0)
            def _():
                s = places[r][which] - 1
                fetch(which, s).wait()
                rows = pl.ds(pl.multiple_of(s * FB, FB), FB)
                for c in range(KB):
                    col = pl.ds(pl.multiple_of(col_ref[which, c] * FB, FB), FB)
                    acc_ref[here, col] += tiles[which, rows, c * FB : (c + 1) * FB]

        store = pltpu.make_async_copy(acc_ref.at[here], ham_hbm.at[here], out_sem.at[r])
        store.start()
        stores.append(store)
    for store in stores:
        store.wait()


def local(devices, density_rows, center_x, center_y, center_z, exponent, brick_blocks):
    params = [x.reshape(-1, 1, FB) for x in (center_x, center_y, center_z, exponent)]
    blocks = brick_blocks.T
    vmem = pl.BlockSpec(memory_space=pltpu.VMEM)
    smem = pl.BlockSpec(memory_space=pltpu.SMEM)
    anywhere = pl.BlockSpec(memory_space=pl.ANY)
    potential, tiles = pl.pallas_call(
        functools.partial(main_kernel, devices),
        out_shape=(
            jax.ShapeDtypeStruct((SIDE, LAYER), f32),
            jax.ShapeDtypeStruct((3, NEAR * FB, KB * FB), f32),
        ),
        in_specs=[smem, anywhere] + [vmem] * 4,
        out_specs=(vmem, anywhere),
        scratch_shapes=[
            pltpu.VMEM((BLK_DEV, 5 * BLK_DEV, FB, FB), bf16),
            pltpu.VMEM((KB * FB, CELLS), bf16),
            pltpu.VMEM((KB * FB, CELLS), bf16),
            pltpu.VMEM((NEAR * FB, KB * FB), bf16),
            pltpu.VMEM((BOTH * FB, KB * FB), bf16),
            pltpu.VMEM((NEAR * FB, KB * FB), bf16),
            pltpu.VMEM((NEAR * FB, KB * FB), bf16),
            pltpu.VMEM((NEAR * FB, CELLS), bf16),
            pltpu.VMEM((BOTH * FB, CELLS), bf16),
            pltpu.VMEM((NEAR * FB, KB * FB), f32),
            pltpu.VMEM((BOTH * FB, KB * FB), f32),
            pltpu.VMEM((LAYER, FB), f32),
            pltpu.VMEM((3 * SIDE, SIDE * FB), bf16),
            pltpu.VMEM((2, SIDE, LAYER), f32),
            pltpu.VMEM((2, SIDE, LAYER), f32),
            pltpu.VMEM((1, 1, FB), f32),
            pltpu.VMEM((2, SIDE, LAYER), f32),
            pltpu.VMEM((2, 8, LAYER), f32),
            pltpu.VMEM((2, 8, LAYER), f32),
            pltpu.VMEM((devices - 1, 1, FB), f32),
            pltpu.SMEM((3, KB), jnp.int32),
            pltpu.SMEM((3, KB), jnp.int32),
            pltpu.SemaphoreType.DMA,
            pltpu.SemaphoreType.DMA((2,)),
            pltpu.SemaphoreType.DMA((5,)),
            pltpu.SemaphoreType.DMA((5,)),
            pltpu.SemaphoreType.DMA((2,)),
            pltpu.SemaphoreType.DMA((2,)),
            pltpu.SemaphoreType.DMA((3,)),
            pltpu.SemaphoreType.DMA((3,)),
        ],
        compiler_params=pltpu.CompilerParams(collective_id=0, has_side_effects=True, vmem_limit_bytes=VMEM_BYTES),
        name="build_tiles",
    )(blocks, density_rows.reshape(BLK_DEV, FB, COLS), *params)
    return pl.pallas_call(
        functools.partial(out_kernel, devices),
        out_shape=(jax.ShapeDtypeStruct((1, CELLS), f32), jax.ShapeDtypeStruct((ROWS, COLS), f32)),
        in_specs=[smem, vmem, anywhere],
        out_specs=(vmem, anywhere),
        scratch_shapes=[
            pltpu.VMEM((ROWS, COLS), f32),
            pltpu.VMEM((3, NEAR * FB, KB * FB), f32),
            pltpu.SMEM((3, KB), jnp.int32),
            pltpu.SMEM((3, KB), jnp.int32),
            pltpu.SemaphoreType.DMA((3, CAP)),
            pltpu.SemaphoreType.DMA((BLK_DEV,)),
        ],
        compiler_params=pltpu.CompilerParams(vmem_limit_bytes=VMEM_BYTES),
        name="place_tiles",
    )(blocks, potential, tiles)


def solution(mesh):
    placed = (P("dev", None), P(), P(), P(), P(), P())
    return jax.shard_map(
        functools.partial(local, mesh.shape["dev"]),
        mesh=mesh,
        in_specs=placed,
        out_specs=(P("dev", None), P("dev", None)),
        check_vma=False,
    )
```

```python
import functools
import math

import jax
import jax.numpy as jnp
from jax import lax
from jax.experimental import pallas as pl
from jax.experimental.pallas import tpu as pltpu
from jax.sharding import PartitionSpec as P

FB = 128
KB = 8
CAP = 4
BLK_DEV = 6
SIDE = 16
LAYER = SIDE * SIDE
CELLS = SIDE * SIDE * SIDE
COLS = 5 * BLK_DEV * FB
ROWS = BLK_DEV * FB
PAIR = 2 * FB
NEAR = 4
BOTH = 6
CHUNK = 4 * LAYER
VMEM_BYTES = 46 * 1024 * 1024

omega = 2.0 / 3.0
four_pi = 4.0 * math.pi
slater = (3.0 / math.pi) ** (1.0 / 3.0)
f32 = jnp.float32
bf16 = jnp.bfloat16


def wrapped(distance):
    moved = distance + 0.5
    return (moved - jnp.floor(moved)) - 0.5


SORT = (
    ((0, 1), (2, 3), (4, 5), (6, 7)),
    ((0, 2), (1, 3), (4, 6), (5, 7)),
    ((1, 2), (5, 6)),
    ((0, 4), (1, 5), (2, 6), (3, 7)),
    ((2, 4), (3, 5)),
    ((1, 2), (3, 4), (5, 6)),
)


def order_blocks(which, brick, first, second, me, devices, bb_ref, slot_ref, col_ref):
    keys = []
    for j in range(KB):
        block = bb_ref[j, brick]
        owner = lax.div(block, BLK_DEV)
        rank = jnp.where(owner == first, 0, jnp.where(owner == second, 1 << 20, 2 << 20))
        keys.append(rank + (owner * 8 + (block - owner * BLK_DEV)))
    for layer in SORT:
        for i, j in layer:
            keys[i], keys[j] = jnp.minimum(keys[i], keys[j]), jnp.maximum(keys[i], keys[j])
    for s, key in enumerate(keys):
        code = key & ((1 << 20) - 1)
        owner = code >> 3
        local = code & 7
        step = owner - me + 2
        step = jnp.where(step < 0, step + devices, jnp.where(step >= devices, step - devices, step))
        slot_ref[which, s] = owner * BLK_DEV + local
        col_ref[which, s] = jnp.minimum(step, 4) * BLK_DEV + local


def pair_of(me):
    return me + 1 - 2 * lax.rem(me, 2)


def across_of(me, devices):
    return lax.rem(me + 2 * lax.rem(me, 2) - 1 + devices, devices)


def factors(block, brick, devices, param_refs):
    point = (lax.broadcasted_iota(jnp.int32, (SIDE, FB), 0).astype(f32) + 0.5) / SIDE
    owner = lax.div(block, BLK_DEV)
    offset = (lax.rem(brick - owner + 1 + devices, devices) - 1).astype(f32)
    mid_x, mid_y, mid_z, rate = [ref[block] for ref in param_refs]
    rate = -rate
    along_x = (offset + point) - mid_x
    along_y = wrapped(point - mid_y)
    along_z = wrapped(point - mid_z)
    return jnp.exp(rate * along_x * along_x), jnp.exp(rate * along_y * along_y), jnp.exp(rate * along_z * along_z)


def plane(factor_y, factor_z, rows_ref):
    for j in range(SIDE):
        rows_ref[j * SIDE : (j + 1) * SIDE, :] = factor_y[j : j + 1] * factor_z
    return rows_ref[...].T


def spread_matrix(spread_ref):
    shape = spread_ref.shape
    source = lax.rem(lax.broadcasted_iota(jnp.int32, shape, 0), SIDE)
    target = lax.broadcasted_iota(jnp.int32, shape, 1) // FB
    spread_ref[...] = jnp.where(source == target, 1.0, 0.0).astype(bf16)


def fill_block(which, a, brick, devices, slot_ref, param_refs, rows_ref, spread_ref, orb_ref):
    factor_x, factor_y, factor_z = factors(slot_ref[which, a], brick, devices, param_refs)
    high = factor_x.astype(bf16)
    rest = factor_x - high.astype(f32)
    middle = rest.astype(bf16)
    low = (rest - middle.astype(f32)).astype(bf16)
    parts = jnp.concatenate([high, middle, low], axis=0)
    factor_yz = plane(factor_y, factor_z, rows_ref)
    start = pl.multiple_of(a * FB, FB)
    for n in range(SIDE // 2):
        wide = lax.dot_general(
            parts,
            spread_ref[:, n * PAIR : (n + 1) * PAIR],
            (((0,), (0,)), ((), ())),
            preferred_element_type=f32,
        )
        for h in range(2):
            one = wide[:, h * FB : (h + 1) * FB]
            i = 2 * n + h
            orb_ref[pl.ds(start, FB), i * LAYER : (i + 1) * LAYER] = jnp.concatenate(
                [one * factor_yz[:, :FB], one * factor_yz[:, FB:]], axis=1
            ).astype(bf16)


def fill_lanes(which, a, brick, devices, slot_ref, param_refs, rows_ref, orb_ref):
    factor_x, factor_y, factor_z = factors(slot_ref[which, a], brick, devices, param_refs)
    along = factor_x.T
    factor_yz = plane(factor_y, factor_z, rows_ref)
    start = pl.multiple_of(a * FB, FB)
    for i in range(SIDE):
        orb_ref[pl.ds(start, FB), i * LAYER : (i + 1) * LAYER] = (along[:, i : i + 1] * factor_yz).astype(bf16)


def fold(mat_ref, pairs):
    for i in range(pairs):
        for j in range(i + 1, pairs):
            above = mat_ref[i * PAIR : (i + 1) * PAIR, j * PAIR : (j + 1) * PAIR].astype(f32)
            below = mat_ref[j * PAIR : (j + 1) * PAIR, i * PAIR : (i + 1) * PAIR].astype(f32)
            mat_ref[i * PAIR : (i + 1) * PAIR, j * PAIR : (j + 1) * PAIR] = (above + below.T).astype(bf16)


def density_chunk(j, pairs, mat_ref, orb_ref, pd_ref, t):
    cells = pl.ds(pl.multiple_of(j * CHUNK, CHUNK), CHUNK)
    total = jnp.zeros((1, CHUNK), f32)
    for i in range(pairs):
        applied = jnp.dot(
            mat_ref[i * PAIR : (i + 1) * PAIR, i * PAIR :], orb_ref[i * PAIR :, cells], preferred_element_type=f32
        )
        own = orb_ref[i * PAIR : (i + 1) * PAIR, cells].astype(f32)
        total = total + jnp.sum(own * applied, axis=0, keepdims=True)
    for q in range(CHUNK // LAYER):
        pd_ref[t, pl.ds(j * (CHUNK // LAYER) + q, 1), :] = total[:, q * LAYER : (q + 1) * LAYER]


def weigh_block(k, orb_ref, pot_ref, t, wei_ref):
    rows = pl.ds(pl.multiple_of(k * FB, FB), FB)
    for i in range(SIDE):
        cells = slice(i * LAYER, (i + 1) * LAYER)
        level = pot_ref[t, i : i + 1, :] * (64.0 / CELLS)
        wei_ref[rows, cells] = (orb_ref[rows, cells].astype(f32) * level).astype(bf16)


def ham_tile(rows, j, wei_ref, orb_ref):
    here = slice(j * PAIR, (j + 1) * PAIR)
    return lax.dot_general(wei_ref[rows, :], orb_ref[here, :], (((1,), (1,)), ((), ())), preferred_element_type=f32)


def ham_column(j, pairs, wei_ref, orb_ref, tile_ref):
    rows = slice(0, PAIR * min(j + 1, pairs))
    here = slice(j * PAIR, (j + 1) * PAIR)
    tile = ham_tile(rows, j, wei_ref, orb_ref)
    tile_ref[rows, here] = tile
    if j < pairs:
        for i in range(j):
            tile_ref[here, i * PAIR : (i + 1) * PAIR] = tile[i * PAIR : (i + 1) * PAIR].T


def potential_of(density, before, after, average):
    scale = omega * four_pi / 6.0
    lane = lax.broadcasted_iota(jnp.int32, (SIDE, LAYER), 1) % SIDE
    row = lax.broadcasted_iota(jnp.int32, (SIDE, LAYER), 0)

    def moved(x, steps, axis):
        return pltpu.roll(x, steps % x.shape[axis], axis)

    source = density - average
    one = scale * source
    up = jnp.where(row == 0, scale * (before - average), moved(one, 1, 0))
    down = jnp.where(row == SIDE - 1, scale * (after - average), moved(one, -1, 0))
    beside = up + down + moved(one, SIDE, 1) + moved(one, -SIDE, 1)
    beside = beside + jnp.where(lane == 0, moved(one, 1 - SIDE, 1), moved(one, 1, 1))
    beside = beside + jnp.where(lane == SIDE - 1, moved(one, SIDE - 1, 1), moved(one, -1, 1))
    two = one + omega * ((four_pi * source + beside) / 6.0 - one)
    size = jnp.abs(density)
    safe = jnp.where(size > 0.0, size, 1.0)
    root = jnp.exp(jnp.log(safe) / 3.0)
    root = root - (root - safe / (root * root)) / 3.0
    root = jnp.where(size > 0.0, root, 0.0)
    root = jnp.where(density < 0.0, -root, root)
    return two - slater * root


def main_kernel(
    devices,
    bb_ref,
    rows_hbm,
    cx,
    cy,
    cz,
    ex,
    out_ref,
    orb_a,
    wei_a,
    tile_b,
    tiles_hbm,
    rows_vmem,
    orb_b,
    mat_a,
    mat_b,
    mat_in,
    mat_out,
    wei_b,
    plane_ref,
    spread_ref,
    pd_ref,
    pot_ref,
    sum_ref,
    full_in,
    before_in,
    after_in,
    sums,
    slot_ref,
    col_ref,
    load_sem,
    mat_sem,
    send_sem,
    recv_sem,
    all_sem,
    tile_send,
    tile_recv,
):
    me = lax.axis_index("dev")
    odd = lax.rem(me, 2)
    pair = pair_of(me)
    across = across_of(me, devices)
    barrier = pltpu.get_barrier_semaphore()

    def at(step):
        return lax.rem(me + step + devices, devices)

    def greet(k, carry):
        pl.semaphore_signal(barrier, inc=1, device_id=(at(k),), device_id_type=pl.DeviceIdType.MESH)
        return carry

    def load(c, carry):
        col = pl.ds(pl.multiple_of(c * FB, FB), FB)
        pltpu.make_async_copy(rows_hbm.at[:, :, col], rows_vmem.at[:, c], load_sem).start()
        return carry

    lax.fori_loop(0, 5 * BLK_DEV, load, 0)
    lax.fori_loop(1, devices, greet, 0)

    lists = ((across, me, me), (me, pair, me), (pair, me, pair))
    for which, (brick, first, second) in enumerate(lists):
        order_blocks(which, brick, first, second, me, devices, bb_ref, slot_ref, col_ref)

    params = (cx, cy, cz, ex)
    spread_matrix(spread_ref)

    def fill_a(a, carry):
        for h in range(2):
            fill_block(0, 2 * a + h, across, devices, slot_ref, params, plane_ref.at[h], spread_ref, orb_a)
        return carry

    lax.fori_loop(0, KB // 2, fill_a, 0)
    pltpu.make_async_copy(rows_vmem, rows_vmem, load_sem).wait()

    def gather(which, a, target, other=None):
        block = slot_ref[which, a]
        owner = lax.div(block, BLK_DEV)
        mask = jnp.full((FB, PAIR), (owner == me).astype(f32), f32).astype(bf16)
        row = block - owner * BLK_DEV
        here = slice(a * FB, (a + 1) * FB)
        for c in range(0, KB, 2):
            there = slice(c * FB, (c + 2) * FB)
            tiles = [rows_vmem[row, col_ref[which, c + h]] for h in range(2)]
            tile = jnp.concatenate(tiles, axis=1) * mask
            target[here, there] = tile if other is None else tile + other[here, there]

    for a in range(NEAR):
        gather(2, a, mat_out)
    pl.semaphore_wait(barrier, devices - 1)
    for a in range(NEAR):
        gather(0, a, mat_a)
    give = pltpu.make_async_remote_copy(
        src_ref=mat_out,
        dst_ref=mat_in,
        send_sem=mat_sem.at[0],
        recv_sem=mat_sem.at[1],
        device_id=(pair,),
        device_id_type=pl.DeviceIdType.MESH,
    )
    give.start()
    fold(mat_a, 2)

    def density_a(j, carry):
        for h in range(2):
            fill_lanes(1, 2 * j + h, me, devices, slot_ref, params, plane_ref.at[h], orb_b)
        density_chunk(j, 2, mat_a, orb_a, pd_ref, odd)
        return carry

    def density_b(j, carry):
        density_chunk(j, 3, mat_b, orb_b, pd_ref, 1 - odd)
        return carry

    lax.fori_loop(0, CELLS // CHUNK, density_a, 0)
    give.wait()
    mat_b[0:PAIR, :] = mat_in[0:PAIR, :]
    for a in range(2, NEAR):
        gather(1, a, mat_b, mat_in)
    for a in range(NEAR, BOTH):
        gather(1, a, mat_b)
    fold(mat_b, 3)
    lax.fori_loop(0, CELLS // CHUNK, density_b, 0)
    layer = jnp.sum(pd_ref[0] + pd_ref[1], axis=0, keepdims=True)
    sum_ref[0] = layer[:, :FB] + layer[:, FB:]

    def to_all(k):
        return pltpu.make_async_remote_copy(
            src_ref=sum_ref.at[0],
            dst_ref=sums.at[k - 1],
            send_sem=all_sem.at[0],
            recv_sem=all_sem.at[1],
            device_id=(at(k),),
            device_id_type=pl.DeviceIdType.MESH,
        )

    def start_sum(k, carry):
        to_all(k).start()
        return carry

    low = lax.rem(me - 1 + odd + devices, devices)
    plan = (
        (pd_ref, full_in, across, 0),
        (pd_ref.at[1, pl.ds(8, 8)], before_in.at[odd], lax.rem(low + 2, devices), 1 + odd),
        (pd_ref.at[1, pl.ds(8, 8)], before_in.at[odd], lax.rem(low + 3, devices), 1 + odd),
        (pd_ref.at[0, pl.ds(0, 8)], after_in.at[odd], lax.rem(low - 2 + devices, devices), 3 + odd),
        (pd_ref.at[0, pl.ds(0, 8)], after_in.at[odd], lax.rem(low - 1 + devices, devices), 3 + odd),
    )
    copies = [
        pltpu.make_async_remote_copy(
            src_ref=src,
            dst_ref=dst,
            send_sem=send_sem.at[q],
            recv_sem=recv_sem.at[r],
            device_id=(device,),
            device_id_type=pl.DeviceIdType.MESH,
        )
        for q, (src, dst, device, r) in enumerate(plan)
    ]
    lax.fori_loop(1, devices, start_sum, 0)
    for copy in copies:
        copy.start()
    pltpu.make_async_copy(full_in, full_in, recv_sem.at[0]).wait()
    for s in range(2):
        pltpu.make_async_copy(before_in.at[s], before_in.at[s], recv_sem.at[1 + s]).wait()
        pltpu.make_async_copy(after_in.at[s], after_in.at[s], recv_sem.at[3 + s]).wait()
    pltpu.make_async_copy(sums, sums, all_sem.at[1]).wait()

    total = jnp.sum(sums[...], axis=0) + sum_ref[0]
    average = jnp.sum(total, axis=1, keepdims=True) / (devices * CELLS)
    first = pd_ref[0] + full_in[0]
    second = pd_ref[1] + full_in[1]
    behind = (before_in[0] + before_in[1])[7:]
    ahead = (after_in[0] + after_in[1])[:1]
    pot_ref[0] = potential_of(first, behind, second[:1], average)
    pot_ref[1] = potential_of(second, first[SIDE - 1 :], ahead, average)
    out_ref[...] = pot_ref[1 - odd]

    def weigh_a(k, carry):
        weigh_block(k, orb_a, pot_ref, odd, wei_a)
        return carry

    def weigh_b(k, carry):
        weigh_block(k, orb_b, pot_ref, 1 - odd, wei_b)
        return carry

    lax.fori_loop(0, BOTH, weigh_b, 0)

    def give_tiles(n, cells):
        return pltpu.make_async_remote_copy(
            src_ref=tile_b.at[pl.ds(0, NEAR * FB), cells],
            dst_ref=tiles_hbm.at[:, cells],
            send_sem=tile_send.at[n],
            recv_sem=tile_recv.at[n],
            device_id=(pair,),
            device_id_type=pl.DeviceIdType.MESH,
        )

    gives = [give_tiles(n, pl.ds(n * PAIR, PAIR)) for n in range(4)]
    for j in (3, 2):
        ham_column(j, 2, wei_b, orb_b, tile_b)
        weigh_a(3 - j, 0)
        gives[j].start()
    ham_column(1, 2, wei_b, orb_b, tile_b)
    weigh_a(2, 0)
    gives[1].start()
    ham_column(0, 2, wei_b, orb_b, tile_b)
    gives[0].start()
    weigh_a(3, 0)
    for j in (2, 3):
        tile = ham_tile(slice(2 * PAIR, 3 * PAIR), j, wei_b, orb_b)
        tile_b[2 * PAIR : 3 * PAIR, j * PAIR : (j + 1) * PAIR] = tile
    for i in range(2):
        tile_b[2 * PAIR : 3 * PAIR, i * PAIR : (i + 1) * PAIR] = tile_b[
            i * PAIR : (i + 1) * PAIR, 2 * PAIR : 3 * PAIR
        ].T
    for copy in copies:
        copy.wait_send()
    pltpu.make_async_copy(sums, sums, all_sem.at[0]).wait()
    for copy in gives:
        copy.wait()


def out_kernel(
    devices,
    bb_ref,
    pot_in,
    orb_a,
    wei_a,
    tile_b,
    tiles_hbm,
    pot_out,
    ham_hbm,
    acc_ref,
    tile_a,
    tile_in,
    slot_ref,
    col_ref,
    in_sem,
    early_sem,
    late_sem,
):
    me = lax.axis_index("dev")
    pair = pair_of(me)
    across = across_of(me, devices)
    fetch = pltpu.make_async_copy(tiles_hbm, tile_in, in_sem)
    fetch.start()
    lists = ((across, me, me), (me, pair, me), (pair, me, pair))
    for which, (brick, first, second) in enumerate(lists):
        order_blocks(which, brick, first, second, me, devices, bb_ref, slot_ref, col_ref)
    sources = (tile_a, tile_b, tile_in)
    first_slot = (0, 2, 0)

    def owned(which, s):
        block = slot_ref[which, first_slot[which] + s]
        owner = lax.div(block, BLK_DEV)
        return owner == me, block - owner * BLK_DEV

    def tile_of(ref, row, which, c):
        col = pl.multiple_of(col_ref[which, c] * FB, FB)
        return ref.at[pl.ds(pl.multiple_of(row * FB, FB), FB), pl.ds(col, FB)]

    def add(which):
        for s in range(CAP):
            mine, row = owned(which, s)
            row = jnp.where(mine, row, BLK_DEV)
            start = (first_slot[which] + s) * FB
            for c in range(KB):
                tile_of(acc_ref, row, which, c)[...] += sources[which][start : start + FB, c * FB : (c + 1) * FB]

    odd = lax.rem(me, 2)
    across_rows = [
        sum((slot_ref[0, s] == me * BLK_DEV + r).astype(jnp.int32) for s in range(CAP)) > 0 for r in range(BLK_DEV)
    ]
    free = pl.ds(pl.multiple_of((1 - odd) * 3 * ROWS, FB), 2 * ROWS)
    shared = pl.ds(pl.multiple_of(odd * 2 * ROWS, FB), 3 * ROWS)

    def store(r, cols, sem):
        here = pl.ds(r * FB, FB)
        return pltpu.make_async_copy(acc_ref.at[here, cols], ham_hbm.at[here, cols], sem.at[r])

    for i in range(SIDE):
        pot_out[:, i * LAYER : (i + 1) * LAYER] = pot_in[i : i + 1, :]
    acc_ref[...] = jnp.zeros(acc_ref.shape, f32)
    add(1)
    fetch.wait()
    add(2)
    ham_column(0, 2, wei_a, orb_a, tile_a)
    for r in range(BLK_DEV):
        store(r, free, early_sem).start()

        @pl.when(jnp.logical_not(across_rows[r]))
        def _():
            store(r, shared, late_sem).start()

    for j in range(1, 4):
        ham_column(j, 2, wei_a, orb_a, tile_a)
    add(0)
    for r in range(BLK_DEV):

        @pl.when(across_rows[r])
        def _():
            store(r, shared, late_sem).start()

    for r in range(BLK_DEV):
        store(r, free, early_sem).wait()
        store(r, shared, late_sem).wait()


def local(devices, density_rows, center_x, center_y, center_z, exponent, brick_blocks):
    params = [x.reshape(-1, 1, FB) for x in (center_x, center_y, center_z, exponent)]
    blocks = brick_blocks.T
    vmem = pl.BlockSpec(memory_space=pltpu.VMEM)
    smem = pl.BlockSpec(memory_space=pltpu.SMEM)
    anywhere = pl.BlockSpec(memory_space=pl.ANY)
    potential, orbitals, weighted, tiles, tiles_in = pl.pallas_call(
        functools.partial(main_kernel, devices),
        out_shape=(
            jax.ShapeDtypeStruct((SIDE, LAYER), f32),
            pltpu.VMEM((KB * FB, CELLS), bf16),
            pltpu.VMEM((NEAR * FB, CELLS), bf16),
            pltpu.VMEM((BOTH * FB, KB * FB), f32),
            jax.ShapeDtypeStruct((NEAR * FB, KB * FB), f32),
        ),
        in_specs=[smem, anywhere] + [vmem] * 4,
        out_specs=(vmem, vmem, vmem, vmem, anywhere),
        scratch_shapes=[
            pltpu.VMEM((BLK_DEV, 5 * BLK_DEV, FB, FB), bf16),
            pltpu.VMEM((KB * FB, CELLS), bf16),
            pltpu.VMEM((NEAR * FB, KB * FB), bf16),
            pltpu.VMEM((BOTH * FB, KB * FB), bf16),
            pltpu.VMEM((NEAR * FB, KB * FB), bf16),
            pltpu.VMEM((NEAR * FB, KB * FB), bf16),
            pltpu.VMEM((BOTH * FB, CELLS), bf16),
            pltpu.VMEM((2, LAYER, FB), f32),
            pltpu.VMEM((3 * SIDE, SIDE * FB), bf16),
            pltpu.VMEM((2, SIDE, LAYER), f32),
            pltpu.VMEM((2, SIDE, LAYER), f32),
            pltpu.VMEM((1, 1, FB), f32),
            pltpu.VMEM((2, SIDE, LAYER), f32),
            pltpu.VMEM((2, 8, LAYER), f32),
            pltpu.VMEM((2, 8, LAYER), f32),
            pltpu.VMEM((devices - 1, 1, FB), f32),
            pltpu.SMEM((3, KB), jnp.int32),
            pltpu.SMEM((3, KB), jnp.int32),
            pltpu.SemaphoreType.DMA,
            pltpu.SemaphoreType.DMA((2,)),
            pltpu.SemaphoreType.DMA((5,)),
            pltpu.SemaphoreType.DMA((5,)),
            pltpu.SemaphoreType.DMA((2,)),
            pltpu.SemaphoreType.DMA((4,)),
            pltpu.SemaphoreType.DMA((4,)),
        ],
        compiler_params=pltpu.CompilerParams(collective_id=0, has_side_effects=True, vmem_limit_bytes=VMEM_BYTES),
        name="build_tiles",
    )(blocks, density_rows.reshape(BLK_DEV, FB, COLS), *params)
    held = [pltpu.with_memory_space_constraint(x, pltpu.VMEM) for x in (orbitals, weighted, tiles)]
    return pl.pallas_call(
        functools.partial(out_kernel, devices),
        out_shape=(jax.ShapeDtypeStruct((1, CELLS), f32), jax.ShapeDtypeStruct((ROWS, COLS), f32)),
        in_specs=[smem] + [vmem] * 4 + [anywhere],
        out_specs=(vmem, anywhere),
        scratch_shapes=[
            pltpu.VMEM((ROWS + FB, COLS), f32),
            pltpu.VMEM((NEAR * FB, KB * FB), f32),
            pltpu.VMEM((NEAR * FB, KB * FB), f32),
            pltpu.SMEM((3, KB), jnp.int32),
            pltpu.SMEM((3, KB), jnp.int32),
            pltpu.SemaphoreType.DMA,
            pltpu.SemaphoreType.DMA((BLK_DEV,)),
            pltpu.SemaphoreType.DMA((BLK_DEV,)),
        ],
        compiler_params=pltpu.CompilerParams(vmem_limit_bytes=VMEM_BYTES),
        name="place_tiles",
    )(blocks, potential, *held, tiles_in)


def solution(mesh):
    placed = (P("dev", None), P(), P(), P(), P(), P())
    return jax.shard_map(
        functools.partial(local, mesh.shape["dev"]),
        mesh=mesh,
        in_specs=placed,
        out_specs=(P("dev", None), P("dev", None)),
        check_vma=False,
    )
```

```python
import functools
import math

import jax
import jax.numpy as jnp
from jax import lax
from jax.experimental import pallas as pl
from jax.experimental.pallas import tpu as pltpu
from jax.sharding import PartitionSpec as P

FB = 128
KB = 8
CAP = 4
BLK_DEV = 6
SIDE = 16
LAYER = SIDE * SIDE
CELLS = SIDE * SIDE * SIDE
COLS = 5 * BLK_DEV * FB
ROWS = BLK_DEV * FB
PAIR = 2 * FB
NEAR = 4
BOTH = 6
CHUNK = 4 * LAYER
VMEM_BYTES = 33 * 1024 * 1024

omega = 2.0 / 3.0
four_pi = 4.0 * math.pi
slater = (3.0 / math.pi) ** (1.0 / 3.0)
f32 = jnp.float32
bf16 = jnp.bfloat16


def wrapped(distance):
    moved = distance + 0.5
    return (moved - jnp.floor(moved)) - 0.5


SORT = (
    ((0, 1), (2, 3), (4, 5), (6, 7)),
    ((0, 2), (1, 3), (4, 6), (5, 7)),
    ((1, 2), (5, 6)),
    ((0, 4), (1, 5), (2, 6), (3, 7)),
    ((2, 4), (3, 5)),
    ((1, 2), (3, 4), (5, 6)),
)


def order_blocks(which, brick, first, second, me, devices, bb_ref, slot_ref, col_ref):
    keys = []
    for j in range(KB):
        block = bb_ref[j, brick]
        owner = lax.div(block, BLK_DEV)
        rank = jnp.where(owner == first, 0, jnp.where(owner == second, 1 << 20, 2 << 20))
        keys.append(rank + (owner * 8 + (block - owner * BLK_DEV)))
    for layer in SORT:
        for i, j in layer:
            keys[i], keys[j] = jnp.minimum(keys[i], keys[j]), jnp.maximum(keys[i], keys[j])
    for s, key in enumerate(keys):
        code = key & ((1 << 20) - 1)
        owner = code >> 3
        local = code & 7
        step = owner - me + 2
        step = jnp.where(step < 0, step + devices, jnp.where(step >= devices, step - devices, step))
        slot_ref[which, s] = owner * BLK_DEV + local
        col_ref[which, s] = jnp.minimum(step, 4) * BLK_DEV + local


def pair_of(me):
    return me + 1 - 2 * lax.rem(me, 2)


def across_of(me, devices):
    return lax.rem(me + 2 * lax.rem(me, 2) - 1 + devices, devices)


def factors(block, brick, devices, param_refs):
    point = (lax.broadcasted_iota(jnp.int32, (SIDE, FB), 0).astype(f32) + 0.5) / SIDE
    owner = lax.div(block, BLK_DEV)
    offset = (lax.rem(brick - owner + 1 + devices, devices) - 1).astype(f32)
    mid_x, mid_y, mid_z, rate = [ref[block] for ref in param_refs]
    rate = -rate
    along_x = (offset + point) - mid_x
    along_y = wrapped(point - mid_y)
    along_z = wrapped(point - mid_z)
    return jnp.exp(rate * along_x * along_x), jnp.exp(rate * along_y * along_y), jnp.exp(rate * along_z * along_z)


def plane(factor_y, factor_z, rows_ref):
    for j in range(SIDE):
        rows_ref[j * SIDE : (j + 1) * SIDE, :] = factor_y[j : j + 1] * factor_z
    return rows_ref[...].T


def spread_matrix(spread_ref):
    shape = spread_ref.shape
    source = lax.rem(lax.broadcasted_iota(jnp.int32, shape, 0), SIDE)
    target = lax.broadcasted_iota(jnp.int32, shape, 1) // FB
    spread_ref[...] = jnp.where(source == target, 1.0, 0.0).astype(bf16)


def fill_block(which, a, brick, devices, slot_ref, param_refs, rows_ref, spread_ref, orb_ref):
    factor_x, factor_y, factor_z = factors(slot_ref[which, a], brick, devices, param_refs)
    high = factor_x.astype(bf16)
    rest = factor_x - high.astype(f32)
    middle = rest.astype(bf16)
    low = (rest - middle.astype(f32)).astype(bf16)
    parts = jnp.concatenate([high, middle, low], axis=0)
    factor_yz = plane(factor_y, factor_z, rows_ref)
    start = pl.multiple_of(a * FB, FB)
    for n in range(SIDE // 2):
        wide = lax.dot_general(
            parts,
            spread_ref[:, n * PAIR : (n + 1) * PAIR],
            (((0,), (0,)), ((), ())),
            preferred_element_type=f32,
        )
        for h in range(2):
            one = wide[:, h * FB : (h + 1) * FB]
            i = 2 * n + h
            orb_ref[pl.ds(start, FB), i * LAYER : (i + 1) * LAYER] = jnp.concatenate(
                [one * factor_yz[:, :FB], one * factor_yz[:, FB:]], axis=1
            ).astype(bf16)


def fill_lanes(which, a, brick, devices, slot_ref, param_refs, rows_ref, orb_ref):
    factor_x, factor_y, factor_z = factors(slot_ref[which, a], brick, devices, param_refs)
    along = factor_x.T
    factor_yz = plane(factor_y, factor_z, rows_ref)
    start = pl.multiple_of(a * FB, FB)
    for i in range(SIDE):
        orb_ref[pl.ds(start, FB), i * LAYER : (i + 1) * LAYER] = (along[:, i : i + 1] * factor_yz).astype(bf16)


def fold(mat_ref, pairs):
    for i in range(pairs):
        for j in range(i + 1, pairs):
            above = mat_ref[i * PAIR : (i + 1) * PAIR, j * PAIR : (j + 1) * PAIR].astype(f32)
            below = mat_ref[j * PAIR : (j + 1) * PAIR, i * PAIR : (i + 1) * PAIR].astype(f32)
            mat_ref[i * PAIR : (i + 1) * PAIR, j * PAIR : (j + 1) * PAIR] = (above + below.T).astype(bf16)


def density_chunk(j, pairs, mat_ref, orb_ref, pd_ref, t):
    cells = pl.ds(pl.multiple_of(j * CHUNK, CHUNK), CHUNK)
    total = jnp.zeros((1, CHUNK), f32)
    for i in range(pairs):
        applied = jnp.dot(
            mat_ref[i * PAIR : (i + 1) * PAIR, i * PAIR :], orb_ref[i * PAIR :, cells], preferred_element_type=f32
        )
        own = orb_ref[i * PAIR : (i + 1) * PAIR, cells].astype(f32)
        total = total + jnp.sum(own * applied, axis=0, keepdims=True)
    for q in range(CHUNK // LAYER):
        pd_ref[t, pl.ds(j * (CHUNK // LAYER) + q, 1), :] = total[:, q * LAYER : (q + 1) * LAYER]


def weigh_block(k, orb_ref, pot_ref, t, wei_ref):
    rows = pl.ds(pl.multiple_of(k * FB, FB), FB)
    for i in range(SIDE):
        cells = slice(i * LAYER, (i + 1) * LAYER)
        level = pot_ref[t, i : i + 1, :] * (64.0 / CELLS)
        wei_ref[rows, cells] = (orb_ref[rows, cells].astype(f32) * level).astype(bf16)


def ham_tile(rows, j, wei_ref, orb_ref):
    here = slice(j * PAIR, (j + 1) * PAIR)
    return lax.dot_general(wei_ref[rows, :], orb_ref[here, :], (((1,), (1,)), ((), ())), preferred_element_type=f32)


def ham_column(j, pairs, wei_ref, orb_ref, tile_ref):
    rows = slice(0, PAIR * min(j + 1, pairs))
    here = slice(j * PAIR, (j + 1) * PAIR)
    tile = ham_tile(rows, j, wei_ref, orb_ref)
    tile_ref[rows, here] = tile
    if j < pairs:
        for i in range(j):
            tile_ref[here, i * PAIR : (i + 1) * PAIR] = tile[i * PAIR : (i + 1) * PAIR].T


def potential_of(density, before, after, average):
    scale = omega * four_pi / 6.0
    lane = lax.broadcasted_iota(jnp.int32, (SIDE, LAYER), 1) % SIDE
    row = lax.broadcasted_iota(jnp.int32, (SIDE, LAYER), 0)

    def moved(x, steps, axis):
        return pltpu.roll(x, steps % x.shape[axis], axis)

    source = density - average
    one = scale * source
    up = jnp.where(row == 0, scale * (before - average), moved(one, 1, 0))
    down = jnp.where(row == SIDE - 1, scale * (after - average), moved(one, -1, 0))
    beside = up + down + moved(one, SIDE, 1) + moved(one, -SIDE, 1)
    beside = beside + jnp.where(lane == 0, moved(one, 1 - SIDE, 1), moved(one, 1, 1))
    beside = beside + jnp.where(lane == SIDE - 1, moved(one, SIDE - 1, 1), moved(one, -1, 1))
    two = one + omega * ((four_pi * source + beside) / 6.0 - one)
    size = jnp.abs(density)
    safe = jnp.where(size > 0.0, size, 1.0)
    root = jnp.exp(jnp.log(safe) / 3.0)
    root = root - (root - safe / (root * root)) / 3.0
    root = jnp.where(size > 0.0, root, 0.0)
    root = jnp.where(density < 0.0, -root, root)
    return two - slater * root


def main_kernel(
    devices,
    bb_ref,
    rows_hbm,
    cx,
    cy,
    cz,
    ex,
    out_ref,
    orb_a,
    wei_a,
    tile_b,
    corner,
    acc_ref,
    tiles_hbm,
    rows_vmem,
    orb_b,
    mat_a,
    mat_b,
    mat_in,
    mat_out,
    wei_b,
    plane_ref,
    spread_ref,
    pd_ref,
    pot_ref,
    sum_ref,
    full_in,
    before_in,
    after_in,
    sums,
    slot_ref,
    col_ref,
    load_sem,
    mat_sem,
    send_sem,
    recv_sem,
    all_sem,
    tile_send,
    tile_recv,
):
    me = lax.axis_index("dev")
    odd = lax.rem(me, 2)
    pair = pair_of(me)
    across = across_of(me, devices)
    barrier = pltpu.get_barrier_semaphore()

    def at(step):
        return lax.rem(me + step + devices, devices)

    def greet(k, carry):
        pl.semaphore_signal(barrier, inc=1, device_id=(at(k),), device_id_type=pl.DeviceIdType.MESH)
        return carry

    def load(c, carry):
        col = pl.ds(pl.multiple_of(c * FB, FB), FB)
        pltpu.make_async_copy(rows_hbm.at[:, :, col], rows_vmem.at[:, c], load_sem).start()
        return carry

    lax.fori_loop(0, 5 * BLK_DEV, load, 0)
    lax.fori_loop(1, devices, greet, 0)

    lists = ((across, me, me), (me, pair, me), (pair, me, pair))
    for which, (brick, first, second) in enumerate(lists):
        order_blocks(which, brick, first, second, me, devices, bb_ref, slot_ref, col_ref)

    params = (cx, cy, cz, ex)
    spread_matrix(spread_ref)

    def fill_a(a, carry):
        for h in range(2):
            fill_block(0, 2 * a + h, across, devices, slot_ref, params, plane_ref.at[h], spread_ref, orb_a)
        return carry

    lax.fori_loop(0, KB // 2, fill_a, 0)
    pltpu.make_async_copy(rows_vmem, rows_vmem, load_sem).wait()

    def gather(which, a, target, other=None):
        block = slot_ref[which, a]
        owner = lax.div(block, BLK_DEV)
        mask = jnp.full((FB, PAIR), (owner == me).astype(f32), f32).astype(bf16)
        row = block - owner * BLK_DEV
        here = slice(a * FB, (a + 1) * FB)
        for c in range(0, KB, 2):
            there = slice(c * FB, (c + 2) * FB)
            tiles = [rows_vmem[row, col_ref[which, c + h]] for h in range(2)]
            tile = jnp.concatenate(tiles, axis=1) * mask
            target[here, there] = tile if other is None else tile + other[here, there]

    for a in range(NEAR):
        gather(2, a, mat_out)
    for a in range(NEAR):
        gather(0, a, mat_a)
    give = pltpu.make_async_remote_copy(
        src_ref=mat_out,
        dst_ref=mat_in,
        send_sem=mat_sem.at[0],
        recv_sem=mat_sem.at[1],
        device_id=(pair,),
        device_id_type=pl.DeviceIdType.MESH,
    )
    fold(mat_a, 2)

    def density_a(j, carry):
        for h in range(2):
            fill_lanes(1, 2 * j + h, me, devices, slot_ref, params, plane_ref.at[h], orb_b)
        density_chunk(j, 2, mat_a, orb_a, pd_ref, odd)
        return carry

    def density_b(j, carry):
        density_chunk(j, 3, mat_b, orb_b, pd_ref, 1 - odd)
        return carry

    lax.fori_loop(0, 1, density_a, 0)
    pl.semaphore_wait(barrier, devices - 1)
    give.start()
    lax.fori_loop(1, CELLS // CHUNK, density_a, 0)
    give.wait()
    mat_b[0:PAIR, :] = mat_in[0:PAIR, :]
    for a in range(2, NEAR):
        gather(1, a, mat_b, mat_in)
    for a in range(NEAR, BOTH):
        gather(1, a, mat_b)
    fold(mat_b, 3)
    lax.fori_loop(0, CELLS // CHUNK, density_b, 0)
    layer = jnp.sum(pd_ref[0] + pd_ref[1], axis=0, keepdims=True)
    sum_ref[0] = layer[:, :FB] + layer[:, FB:]

    def to_all(k):
        return pltpu.make_async_remote_copy(
            src_ref=sum_ref.at[0],
            dst_ref=sums.at[k - 1],
            send_sem=all_sem.at[0],
            recv_sem=all_sem.at[1],
            device_id=(at(k),),
            device_id_type=pl.DeviceIdType.MESH,
        )

    def start_sum(k, carry):
        to_all(k).start()
        return carry

    low = lax.rem(me - 1 + odd + devices, devices)
    plan = (
        (pd_ref, full_in, across, 0),
        (pd_ref.at[1, pl.ds(8, 8)], before_in.at[odd], lax.rem(low + 2, devices), 1 + odd),
        (pd_ref.at[1, pl.ds(8, 8)], before_in.at[odd], lax.rem(low + 3, devices), 1 + odd),
        (pd_ref.at[0, pl.ds(0, 8)], after_in.at[odd], lax.rem(low - 2 + devices, devices), 3 + odd),
        (pd_ref.at[0, pl.ds(0, 8)], after_in.at[odd], lax.rem(low - 1 + devices, devices), 3 + odd),
    )
    copies = [
        pltpu.make_async_remote_copy(
            src_ref=src,
            dst_ref=dst,
            send_sem=send_sem.at[q],
            recv_sem=recv_sem.at[r],
            device_id=(device,),
            device_id_type=pl.DeviceIdType.MESH,
        )
        for q, (src, dst, device, r) in enumerate(plan)
    ]
    lax.fori_loop(1, devices, start_sum, 0)
    for copy in copies:
        copy.start()
    acc_ref[...] = jnp.zeros(acc_ref.shape, f32)
    pltpu.make_async_copy(full_in, full_in, recv_sem.at[0]).wait()
    for s in range(2):
        pltpu.make_async_copy(before_in.at[s], before_in.at[s], recv_sem.at[1 + s]).wait()
        pltpu.make_async_copy(after_in.at[s], after_in.at[s], recv_sem.at[3 + s]).wait()
    pltpu.make_async_copy(sums, sums, all_sem.at[1]).wait()

    total = jnp.sum(sums[...], axis=0) + sum_ref[0]
    average = jnp.sum(total, axis=1, keepdims=True) / (devices * CELLS)
    first = pd_ref[0] + full_in[0]
    second = pd_ref[1] + full_in[1]
    behind = (before_in[0] + before_in[1])[7:]
    ahead = (after_in[0] + after_in[1])[:1]
    pot_ref[0] = potential_of(first, behind, second[:1], average)
    pot_ref[1] = potential_of(second, first[SIDE - 1 :], ahead, average)
    out_ref[...] = pot_ref[1 - odd]

    def weigh_a(k, carry):
        weigh_block(k, orb_a, pot_ref, odd, wei_a)
        return carry

    def weigh_b(k, carry):
        weigh_block(k, orb_b, pot_ref, 1 - odd, wei_b)
        return carry

    lax.fori_loop(0, BOTH, weigh_b, 0)

    def give_tiles(n, cells):
        return pltpu.make_async_remote_copy(
            src_ref=tile_b.at[pl.ds(0, NEAR * FB), cells],
            dst_ref=tiles_hbm.at[:, cells],
            send_sem=tile_send.at[n],
            recv_sem=tile_recv.at[n],
            device_id=(pair,),
            device_id_type=pl.DeviceIdType.MESH,
        )

    gives = [give_tiles(n, pl.ds(n * 2 * PAIR, 2 * PAIR)) for n in range(2)]
    for j in (3, 2):
        ham_column(j, 2, wei_b, orb_b, tile_b)
        weigh_a(3 - j, 0)
    gives[1].start()
    for j in (1, 0):
        ham_column(j, 2, wei_b, orb_b, tile_b)
        weigh_a(3 - j, 0)
    gives[0].start()
    last = slice(2 * PAIR, 3 * PAIR)
    for j in (2, 3):
        tile_b[last, j * PAIR : (j + 1) * PAIR] = ham_tile(last, j, wei_b, orb_b)
    for i in range(2):
        tile_b[last, i * PAIR : (i + 1) * PAIR] = tile_b[i * PAIR : (i + 1) * PAIR, last].T
    corner[...] = ham_tile(slice(0, PAIR), 0, wei_a, orb_a)
    for copy in copies:
        copy.wait_send()
    pltpu.make_async_copy(sums, sums, all_sem.at[0]).wait()
    for copy in gives:
        copy.wait()


def out_kernel(
    devices,
    bb_hbm,
    pot_in,
    orb_a,
    wei_a,
    tile_b,
    corner,
    acc_in,
    tiles_hbm,
    pot_out,
    ham_hbm,
    acc_ref,
    tile_a,
    tile_in,
    bb_ref,
    slot_ref,
    col_ref,
    in_sem,
    bb_sem,
    early_sem,
    late_sem,
):
    me = lax.axis_index("dev")
    pair = pair_of(me)
    across = across_of(me, devices)
    lay = pltpu.make_async_copy(bb_hbm, bb_ref, bb_sem)
    lay.start()
    fetch = pltpu.make_async_copy(tiles_hbm, tile_in, in_sem)
    fetch.start()
    for i in range(SIDE):
        pot_out[:, i * LAYER : (i + 1) * LAYER] = pot_in[i : i + 1, :]
    tile_a[0:PAIR, 0:PAIR] = corner[...]
    lay.wait()
    lists = ((across, me, me), (me, pair, me), (pair, me, pair))
    for which, (brick, first, second) in enumerate(lists):
        order_blocks(which, brick, first, second, me, devices, bb_ref, slot_ref, col_ref)
    sources = (tile_a, tile_b, tile_in)
    first_slot = (0, 2, 0)

    def owned(which, s):
        block = slot_ref[which, first_slot[which] + s]
        owner = lax.div(block, BLK_DEV)
        return owner == me, block - owner * BLK_DEV

    def tile_of(ref, row, which, c):
        col = pl.multiple_of(col_ref[which, c] * FB, FB)
        return ref.at[pl.ds(pl.multiple_of(row * FB, FB), FB), pl.ds(col, FB)]

    def add(which):
        for s in range(CAP):
            mine, row = owned(which, s)
            row = jnp.where(mine, row, BLK_DEV)
            start = (first_slot[which] + s) * FB
            for c in range(KB):
                tile_of(acc_ref, row, which, c)[...] += sources[which][start : start + FB, c * FB : (c + 1) * FB]

    across_rows = [
        sum((slot_ref[0, s] == me * BLK_DEV + r).astype(jnp.int32) for s in range(CAP)) > 0 for r in range(BLK_DEV)
    ]

    def store_row(r):
        here = pl.ds(r * FB, FB)
        return pltpu.make_async_copy(acc_ref.at[here], ham_hbm.at[here], early_sem.at[r])

    def each_tile(act):
        for s in range(CAP):
            mine, row = owned(0, s)

            @pl.when(mine)
            def _():
                for c in range(KB):
                    source, target = tile_of(acc_ref, row, 0, c), tile_of(ham_hbm, row, 0, c)
                    act(pltpu.make_async_copy(source, target, late_sem.at[s, c]))

    odd = lax.rem(me, 2)
    free = pl.ds(pl.multiple_of((1 - odd) * 3 * ROWS, FB), 2 * ROWS)
    shared = pl.ds(pl.multiple_of(odd * 2 * ROWS, FB), 3 * ROWS)

    def store(r, cols, sem):
        here = pl.ds(r * FB, FB)
        return pltpu.make_async_copy(acc_ref.at[here, cols], ham_hbm.at[here, cols], sem.at[r])

    add(1)
    fetch.wait()
    add(2)
    for r in range(BLK_DEV):
        store(r, free, early_sem).start()

        @pl.when(jnp.logical_not(across_rows[r]))
        def _():
            store(r, shared, late_sem).start()

    for j in range(1, 4):
        ham_column(j, 2, wei_a, orb_a, tile_a)
    add(0)
    for r in range(BLK_DEV):

        @pl.when(across_rows[r])
        def _():
            store(r, shared, late_sem).start()

    for r in range(BLK_DEV):
        store(r, free, early_sem).wait()
        store(r, shared, late_sem).wait()


def local(devices, density_rows, center_x, center_y, center_z, exponent, brick_blocks):
    params = [x.reshape(-1, 1, FB) for x in (center_x, center_y, center_z, exponent)]
    blocks = brick_blocks.T
    vmem = pl.BlockSpec(memory_space=pltpu.VMEM)
    smem = pl.BlockSpec(memory_space=pltpu.SMEM)
    anywhere = pl.BlockSpec(memory_space=pl.ANY)
    *held, tiles_in = pl.pallas_call(
        functools.partial(main_kernel, devices),
        out_shape=(
            pltpu.VMEM((SIDE, LAYER), f32),
            pltpu.VMEM((KB * FB, CELLS), bf16),
            pltpu.VMEM((NEAR * FB, CELLS), bf16),
            pltpu.VMEM((BOTH * FB, KB * FB), f32),
            pltpu.VMEM((PAIR, PAIR), f32),
            pltpu.VMEM((ROWS + FB, COLS), f32),
            jax.ShapeDtypeStruct((NEAR * FB, KB * FB), f32),
        ),
        in_specs=[smem, anywhere] + [vmem] * 4,
        out_specs=(vmem,) * 6 + (anywhere,),
        scratch_shapes=[
            pltpu.VMEM((BLK_DEV, 5 * BLK_DEV, FB, FB), bf16),
            pltpu.VMEM((KB * FB, CELLS), bf16),
            pltpu.VMEM((NEAR * FB, KB * FB), bf16),
            pltpu.VMEM((BOTH * FB, KB * FB), bf16),
            pltpu.VMEM((NEAR * FB, KB * FB), bf16),
            pltpu.VMEM((NEAR * FB, KB * FB), bf16),
            pltpu.VMEM((BOTH * FB, CELLS), bf16),
            pltpu.VMEM((2, LAYER, FB), f32),
            pltpu.VMEM((3 * SIDE, SIDE * FB), bf16),
            pltpu.VMEM((2, SIDE, LAYER), f32),
            pltpu.VMEM((2, SIDE, LAYER), f32),
            pltpu.VMEM((1, 1, FB), f32),
            pltpu.VMEM((2, SIDE, LAYER), f32),
            pltpu.VMEM((2, 8, LAYER), f32),
            pltpu.VMEM((2, 8, LAYER), f32),
            pltpu.VMEM((devices - 1, 1, FB), f32),
            pltpu.SMEM((3, KB), jnp.int32),
            pltpu.SMEM((3, KB), jnp.int32),
            pltpu.SemaphoreType.DMA,
            pltpu.SemaphoreType.DMA((2,)),
            pltpu.SemaphoreType.DMA((5,)),
            pltpu.SemaphoreType.DMA((5,)),
            pltpu.SemaphoreType.DMA((2,)),
            pltpu.SemaphoreType.DMA((2,)),
            pltpu.SemaphoreType.DMA((2,)),
        ],
        compiler_params=pltpu.CompilerParams(collective_id=0, has_side_effects=True, vmem_limit_bytes=VMEM_BYTES),
        name="build_tiles",
    )(blocks, density_rows.reshape(BLK_DEV, FB, COLS), *params)
    held = [pltpu.with_memory_space_constraint(x, pltpu.VMEM) for x in held]
    potential, ham, _ = pl.pallas_call(
        functools.partial(out_kernel, devices),
        out_shape=(
            jax.ShapeDtypeStruct((1, CELLS), f32),
            jax.ShapeDtypeStruct((ROWS, COLS), f32),
            pltpu.VMEM((ROWS + FB, COLS), f32),
        ),
        in_specs=[anywhere] + [vmem] * 6 + [anywhere],
        out_specs=(vmem, anywhere, vmem),
        input_output_aliases={6: 2},
        scratch_shapes=[
            pltpu.VMEM((NEAR * FB, KB * FB), f32),
            pltpu.VMEM((NEAR * FB, KB * FB), f32),
            pltpu.SMEM((KB, devices), jnp.int32),
            pltpu.SMEM((3, KB), jnp.int32),
            pltpu.SMEM((3, KB), jnp.int32),
            pltpu.SemaphoreType.DMA,
            pltpu.SemaphoreType.DMA,
            pltpu.SemaphoreType.DMA((BLK_DEV,)),
            pltpu.SemaphoreType.DMA((BLK_DEV,)),
        ],
        compiler_params=pltpu.CompilerParams(vmem_limit_bytes=VMEM_BYTES),
        name="place_tiles",
    )(blocks, *held, tiles_in)
    return potential, ham


def solution(mesh):
    placed = (P("dev", None), P(), P(), P(), P(), P())
    return jax.shard_map(
        functools.partial(local, mesh.shape["dev"]),
        mesh=mesh,
        in_specs=placed,
        out_specs=(P("dev", None), P("dev", None)),
        check_vma=False,
    )
```

```python
import functools
import math

import jax
import jax.numpy as jnp
from jax import lax
from jax.experimental import pallas as pl
from jax.experimental.pallas import tpu as pltpu
from jax.sharding import PartitionSpec as P

FB = 128
KB = 8
CAP = 4
BLK_DEV = 6
SIDE = 16
LAYER = SIDE * SIDE
CELLS = SIDE * SIDE * SIDE
COLS = 5 * BLK_DEV * FB
ROWS = BLK_DEV * FB
PAIR = 2 * FB
NEAR = 4
BOTH = 6
CHUNK = 4 * LAYER
VMEM_BYTES = 33 * 1024 * 1024

omega = 2.0 / 3.0
four_pi = 4.0 * math.pi
slater = (3.0 / math.pi) ** (1.0 / 3.0)
f32 = jnp.float32
bf16 = jnp.bfloat16


def wrapped(distance):
    moved = distance + 0.5
    return (moved - jnp.floor(moved)) - 0.5


SORT = (
    ((0, 1), (2, 3), (4, 5), (6, 7)),
    ((0, 2), (1, 3), (4, 6), (5, 7)),
    ((1, 2), (5, 6)),
    ((0, 4), (1, 5), (2, 6), (3, 7)),
    ((2, 4), (3, 5)),
    ((1, 2), (3, 4), (5, 6)),
)


def order_blocks(which, brick, first, second, me, devices, bb_ref, slot_ref):
    keys = []
    for j in range(KB):
        block = bb_ref[j, brick]
        owner = lax.div(block, BLK_DEV)
        rank = jnp.where(owner == first, 0, jnp.where(owner == second, 1 << 20, 2 << 20))
        keys.append(rank + (owner * 8 + (block - owner * BLK_DEV)))
    for layer in SORT:
        for i, j in layer:
            keys[i], keys[j] = jnp.minimum(keys[i], keys[j]), jnp.maximum(keys[i], keys[j])
    for s, key in enumerate(keys):
        code = key & ((1 << 20) - 1)
        owner = code >> 3
        local = code & 7
        step = owner - me + 2
        step = jnp.where(step < 0, step + devices, jnp.where(step >= devices, step - devices, step))
        slot_ref[which, s] = owner * BLK_DEV + local
        slot_ref[3 + which, s] = jnp.minimum(step, 4) * BLK_DEV + local


def pair_of(me):
    return me + 1 - 2 * lax.rem(me, 2)


def across_of(me, devices):
    return lax.rem(me + 2 * lax.rem(me, 2) - 1 + devices, devices)


def factors(block, brick, devices, param_refs):
    point = (lax.broadcasted_iota(jnp.int32, (SIDE, FB), 0).astype(f32) + 0.5) / SIDE
    owner = lax.div(block, BLK_DEV)
    offset = (lax.rem(brick - owner + 1 + devices, devices) - 1).astype(f32)
    mid_x, mid_y, mid_z, rate = [ref[block] for ref in param_refs]
    rate = -rate
    along_x = (offset + point) - mid_x
    along_y = wrapped(point - mid_y)
    along_z = wrapped(point - mid_z)
    return jnp.exp(rate * along_x * along_x), jnp.exp(rate * along_y * along_y), jnp.exp(rate * along_z * along_z)


def plane(factor_y, factor_z, rows_ref):
    for j in range(SIDE):
        rows_ref[j * SIDE : (j + 1) * SIDE, :] = factor_y[j : j + 1] * factor_z
    return rows_ref[...].T


def spread_matrix(spread_ref):
    shape = spread_ref.shape
    source = lax.rem(lax.broadcasted_iota(jnp.int32, shape, 0), SIDE)
    target = lax.broadcasted_iota(jnp.int32, shape, 1) // FB
    spread_ref[...] = jnp.where(source == target, 1.0, 0.0).astype(bf16)


def fill_block(which, a, brick, devices, slot_ref, param_refs, rows_ref, spread_ref, orb_ref):
    factor_x, factor_y, factor_z = factors(slot_ref[which, a], brick, devices, param_refs)
    high = factor_x.astype(bf16)
    rest = factor_x - high.astype(f32)
    middle = rest.astype(bf16)
    low = (rest - middle.astype(f32)).astype(bf16)
    parts = jnp.concatenate([high, middle, low], axis=0)
    factor_yz = plane(factor_y, factor_z, rows_ref)
    start = pl.multiple_of(a * FB, FB)
    for n in range(SIDE // 2):
        wide = lax.dot_general(
            parts,
            spread_ref[:, n * PAIR : (n + 1) * PAIR],
            (((0,), (0,)), ((), ())),
            preferred_element_type=f32,
        )
        for h in range(2):
            one = wide[:, h * FB : (h + 1) * FB]
            i = 2 * n + h
            orb_ref[pl.ds(start, FB), i * LAYER : (i + 1) * LAYER] = jnp.concatenate(
                [one * factor_yz[:, :FB], one * factor_yz[:, FB:]], axis=1
            ).astype(bf16)


def fill_lanes(which, a, brick, devices, slot_ref, param_refs, rows_ref, orb_ref):
    factor_x, factor_y, factor_z = factors(slot_ref[which, a], brick, devices, param_refs)
    along = factor_x.T
    factor_yz = plane(factor_y, factor_z, rows_ref)
    start = pl.multiple_of(a * FB, FB)
    for i in range(SIDE):
        orb_ref[pl.ds(start, FB), i * LAYER : (i + 1) * LAYER] = (along[:, i : i + 1] * factor_yz).astype(bf16)


def fold(mat_ref, pairs):
    for i in range(pairs):
        for j in range(i + 1, pairs):
            above = mat_ref[i * PAIR : (i + 1) * PAIR, j * PAIR : (j + 1) * PAIR].astype(f32)
            below = mat_ref[j * PAIR : (j + 1) * PAIR, i * PAIR : (i + 1) * PAIR].astype(f32)
            mat_ref[i * PAIR : (i + 1) * PAIR, j * PAIR : (j + 1) * PAIR] = (above + below.T).astype(bf16)


def density_chunk(j, pairs, mat_ref, orb_ref, pd_ref, t):
    cells = pl.ds(pl.multiple_of(j * CHUNK, CHUNK), CHUNK)
    total = jnp.zeros((1, CHUNK), f32)
    for i in range(pairs):
        applied = jnp.dot(
            mat_ref[i * PAIR : (i + 1) * PAIR, i * PAIR :], orb_ref[i * PAIR :, cells], preferred_element_type=f32
        )
        own = orb_ref[i * PAIR : (i + 1) * PAIR, cells].astype(f32)
        total = total + jnp.sum(own * applied, axis=0, keepdims=True)
    for q in range(CHUNK // LAYER):
        pd_ref[t, pl.ds(j * (CHUNK // LAYER) + q, 1), :] = total[:, q * LAYER : (q + 1) * LAYER]


def weigh_block(k, orb_ref, pot_ref, t, wei_ref):
    rows = pl.ds(pl.multiple_of(k * FB, FB), FB)
    for i in range(SIDE):
        cells = slice(i * LAYER, (i + 1) * LAYER)
        level = pot_ref[t, i : i + 1, :] * (64.0 / CELLS)
        wei_ref[rows, cells] = (orb_ref[rows, cells].astype(f32) * level).astype(bf16)


def ham_tile(rows, j, wei_ref, orb_ref):
    here = slice(j * PAIR, (j + 1) * PAIR)
    return lax.dot_general(wei_ref[rows, :], orb_ref[here, :], (((1,), (1,)), ((), ())), preferred_element_type=f32)


def ham_column(j, pairs, wei_ref, orb_ref, tile_ref):
    rows = slice(0, PAIR * min(j + 1, pairs))
    here = slice(j * PAIR, (j + 1) * PAIR)
    tile = ham_tile(rows, j, wei_ref, orb_ref)
    tile_ref[rows, here] = tile
    if j < pairs:
        for i in range(j):
            tile_ref[here, i * PAIR : (i + 1) * PAIR] = tile[i * PAIR : (i + 1) * PAIR].T


def potential_of(density, before, after, average):
    scale = omega * four_pi / 6.0
    lane = lax.broadcasted_iota(jnp.int32, (SIDE, LAYER), 1) % SIDE
    row = lax.broadcasted_iota(jnp.int32, (SIDE, LAYER), 0)

    def moved(x, steps, axis):
        return pltpu.roll(x, steps % x.shape[axis], axis)

    source = density - average
    one = scale * source
    up = jnp.where(row == 0, scale * (before - average), moved(one, 1, 0))
    down = jnp.where(row == SIDE - 1, scale * (after - average), moved(one, -1, 0))
    beside = up + down + moved(one, SIDE, 1) + moved(one, -SIDE, 1)
    beside = beside + jnp.where(lane == 0, moved(one, 1 - SIDE, 1), moved(one, 1, 1))
    beside = beside + jnp.where(lane == SIDE - 1, moved(one, SIDE - 1, 1), moved(one, -1, 1))
    two = one + omega * ((four_pi * source + beside) / 6.0 - one)
    size = jnp.abs(density)
    safe = jnp.where(size > 0.0, size, 1.0)
    root = jnp.exp(jnp.log(safe) / 3.0)
    root = root - (root - safe / (root * root)) / 3.0
    root = jnp.where(size > 0.0, root, 0.0)
    root = jnp.where(density < 0.0, -root, root)
    return two - slater * root


def main_kernel(
    devices,
    bb_ref,
    rows_hbm,
    cx,
    cy,
    cz,
    ex,
    out_ref,
    orb_a,
    wei_a,
    tile_b,
    corner,
    acc_ref,
    tiles_hbm,
    lists_hbm,
    rows_vmem,
    orb_b,
    mat_a,
    mat_b,
    mat_in,
    mat_out,
    wei_b,
    plane_ref,
    spread_ref,
    pd_ref,
    pot_ref,
    sum_ref,
    full_in,
    before_in,
    after_in,
    sums,
    slot_ref,
    load_sem,
    mat_sem,
    send_sem,
    recv_sem,
    all_sem,
    tile_send,
    tile_recv,
    list_sem,
):
    me = lax.axis_index("dev")
    odd = lax.rem(me, 2)
    pair = pair_of(me)
    across = across_of(me, devices)
    barrier = pltpu.get_barrier_semaphore()

    def at(step):
        return lax.rem(me + step + devices, devices)

    def greet(k, carry):
        pl.semaphore_signal(barrier, inc=1, device_id=(at(k),), device_id_type=pl.DeviceIdType.MESH)
        return carry

    def load(c, carry):
        col = pl.ds(pl.multiple_of(c * FB, FB), FB)
        pltpu.make_async_copy(rows_hbm.at[:, :, col], rows_vmem.at[:, c], load_sem).start()
        return carry

    lax.fori_loop(0, 5 * BLK_DEV, load, 0)
    lax.fori_loop(1, devices, greet, 0)

    lists = ((across, me, me), (me, pair, me), (pair, me, pair))
    for which, (brick, first, second) in enumerate(lists):
        order_blocks(which, brick, first, second, me, devices, bb_ref, slot_ref)

    keep_lists = pltpu.make_async_copy(slot_ref, lists_hbm, list_sem)
    keep_lists.start()
    params = (cx, cy, cz, ex)
    spread_matrix(spread_ref)

    def fill_a(a, carry):
        for h in range(2):
            fill_block(0, 2 * a + h, across, devices, slot_ref, params, plane_ref.at[h], spread_ref, orb_a)
        return carry

    lax.fori_loop(0, KB // 2, fill_a, 0)
    pltpu.make_async_copy(rows_vmem, rows_vmem, load_sem).wait()

    def gather(which, a, target, other=None):
        block = slot_ref[which, a]
        owner = lax.div(block, BLK_DEV)
        mask = jnp.full((FB, PAIR), (owner == me).astype(f32), f32).astype(bf16)
        row = block - owner * BLK_DEV
        here = slice(a * FB, (a + 1) * FB)
        for c in range(0, KB, 2):
            there = slice(c * FB, (c + 2) * FB)
            tiles = [rows_vmem[row, slot_ref[3 + which, c + h]] for h in range(2)]
            tile = jnp.concatenate(tiles, axis=1) * mask
            target[here, there] = tile if other is None else tile + other[here, there]

    for a in range(NEAR):
        gather(2, a, mat_out)
    for a in range(NEAR):
        gather(0, a, mat_a)
    give = pltpu.make_async_remote_copy(
        src_ref=mat_out,
        dst_ref=mat_in,
        send_sem=mat_sem.at[0],
        recv_sem=mat_sem.at[1],
        device_id=(pair,),
        device_id_type=pl.DeviceIdType.MESH,
    )
    fold(mat_a, 2)

    def density_a(j, carry):
        for h in range(2):
            fill_lanes(1, 2 * j + h, me, devices, slot_ref, params, plane_ref.at[h], orb_b)
        density_chunk(j, 2, mat_a, orb_a, pd_ref, odd)
        return carry

    def density_b(j, carry):
        density_chunk(j, 3, mat_b, orb_b, pd_ref, 1 - odd)
        return carry

    lax.fori_loop(0, 1, density_a, 0)
    pl.semaphore_wait(barrier, devices - 1)
    give.start()
    lax.fori_loop(1, CELLS // CHUNK, density_a, 0)
    give.wait()
    mat_b[0:PAIR, :] = mat_in[0:PAIR, :]
    for a in range(2, NEAR):
        gather(1, a, mat_b, mat_in)
    for a in range(NEAR, BOTH):
        gather(1, a, mat_b)
    fold(mat_b, 3)
    lax.fori_loop(0, CELLS // CHUNK, density_b, 0)
    layer = jnp.sum(pd_ref[0] + pd_ref[1], axis=0, keepdims=True)
    sum_ref[0] = layer[:, :FB] + layer[:, FB:]

    def to_all(k):
        return pltpu.make_async_remote_copy(
            src_ref=sum_ref.at[0],
            dst_ref=sums.at[k - 1],
            send_sem=all_sem.at[0],
            recv_sem=all_sem.at[1],
            device_id=(at(k),),
            device_id_type=pl.DeviceIdType.MESH,
        )

    def start_sum(k, carry):
        to_all(k).start()
        return carry

    low = lax.rem(me - 1 + odd + devices, devices)
    plan = (
        (pd_ref, full_in, across, 0),
        (pd_ref.at[1, pl.ds(8, 8)], before_in.at[odd], lax.rem(low + 2, devices), 1 + odd),
        (pd_ref.at[1, pl.ds(8, 8)], before_in.at[odd], lax.rem(low + 3, devices), 1 + odd),
        (pd_ref.at[0, pl.ds(0, 8)], after_in.at[odd], lax.rem(low - 2 + devices, devices), 3 + odd),
        (pd_ref.at[0, pl.ds(0, 8)], after_in.at[odd], lax.rem(low - 1 + devices, devices), 3 + odd),
    )
    copies = [
        pltpu.make_async_remote_copy(
            src_ref=src,
            dst_ref=dst,
            send_sem=send_sem.at[q],
            recv_sem=recv_sem.at[r],
            device_id=(device,),
            device_id_type=pl.DeviceIdType.MESH,
        )
        for q, (src, dst, device, r) in enumerate(plan)
    ]
    lax.fori_loop(1, devices, start_sum, 0)
    for copy in copies:
        copy.start()
    acc_ref[...] = jnp.zeros(acc_ref.shape, f32)
    pltpu.make_async_copy(full_in, full_in, recv_sem.at[0]).wait()
    for s in range(2):
        pltpu.make_async_copy(before_in.at[s], before_in.at[s], recv_sem.at[1 + s]).wait()
        pltpu.make_async_copy(after_in.at[s], after_in.at[s], recv_sem.at[3 + s]).wait()
    pltpu.make_async_copy(sums, sums, all_sem.at[1]).wait()

    total = jnp.sum(sums[...], axis=0) + sum_ref[0]
    average = jnp.sum(total, axis=1, keepdims=True) / (devices * CELLS)
    first = pd_ref[0] + full_in[0]
    second = pd_ref[1] + full_in[1]
    behind = (before_in[0] + before_in[1])[7:]
    ahead = (after_in[0] + after_in[1])[:1]
    pot_ref[0] = potential_of(first, behind, second[:1], average)
    pot_ref[1] = potential_of(second, first[SIDE - 1 :], ahead, average)
    out_ref[...] = pot_ref[1 - odd]

    def weigh_a(k, carry):
        weigh_block(k, orb_a, pot_ref, odd, wei_a)
        return carry

    def weigh_b(k, carry):
        weigh_block(k, orb_b, pot_ref, 1 - odd, wei_b)
        return carry

    lax.fori_loop(0, NEAR, weigh_b, 0)

    def give_tiles(n, cells):
        return pltpu.make_async_remote_copy(
            src_ref=tile_b.at[pl.ds(0, NEAR * FB), cells],
            dst_ref=tiles_hbm.at[:, cells],
            send_sem=tile_send.at[n],
            recv_sem=tile_recv.at[n],
            device_id=(pair,),
            device_id_type=pl.DeviceIdType.MESH,
        )

    gives = [give_tiles(n, pl.ds(n * 2 * PAIR, 2 * PAIR)) for n in range(2)]
    for j in (3, 2):
        ham_column(j, 2, wei_b, orb_b, tile_b)
        weigh_b(NEAR + 3 - j, 0)
        weigh_a(3 - j, 0)
    gives[1].start()
    for j in (1, 0):
        ham_column(j, 2, wei_b, orb_b, tile_b)
        weigh_a(3 - j, 0)
    gives[0].start()
    last = slice(2 * PAIR, 3 * PAIR)
    for j in (2, 3):
        tile_b[last, j * PAIR : (j + 1) * PAIR] = ham_tile(last, j, wei_b, orb_b)
    for i in range(2):
        tile_b[last, i * PAIR : (i + 1) * PAIR] = tile_b[i * PAIR : (i + 1) * PAIR, last].T
    corner[...] = ham_tile(slice(0, PAIR), 0, wei_a, orb_a)
    for copy in copies:
        copy.wait_send()
    pltpu.make_async_copy(sums, sums, all_sem.at[0]).wait()
    for copy in gives:
        copy.wait()
    keep_lists.wait()


def out_kernel(
    devices,
    lists_hbm,
    pot_in,
    orb_a,
    wei_a,
    tile_b,
    corner,
    acc_in,
    tiles_hbm,
    pot_out,
    ham_hbm,
    acc_ref,
    tile_a,
    tile_in,
    slot_ref,
    in_sem,
    list_sem,
    early_sem,
    late_sem,
):
    me = lax.axis_index("dev")
    lay = pltpu.make_async_copy(lists_hbm, slot_ref, list_sem)
    lay.start()
    fetch = pltpu.make_async_copy(tiles_hbm, tile_in, in_sem)
    fetch.start()
    for i in range(SIDE):
        pot_out[:, i * LAYER : (i + 1) * LAYER] = pot_in[i : i + 1, :]
    tile_a[0:PAIR, 0:PAIR] = corner[...]
    lay.wait()
    sources = (tile_a, tile_b, tile_in)
    first_slot = (0, 2, 0)

    def owned(which, s):
        block = slot_ref[which, first_slot[which] + s]
        owner = lax.div(block, BLK_DEV)
        return owner == me, block - owner * BLK_DEV

    def tile_of(ref, row, which, c):
        col = pl.multiple_of(slot_ref[3 + which, c] * FB, FB)
        return ref.at[pl.ds(pl.multiple_of(row * FB, FB), FB), pl.ds(col, FB)]

    def add(which):
        for s in range(CAP):
            mine, row = owned(which, s)
            row = jnp.where(mine, row, BLK_DEV)
            start = (first_slot[which] + s) * FB
            for c in range(KB):
                tile_of(acc_ref, row, which, c)[...] += sources[which][start : start + FB, c * FB : (c + 1) * FB]

    across_rows = [
        sum((slot_ref[0, s] == me * BLK_DEV + r).astype(jnp.int32) for s in range(CAP)) > 0 for r in range(BLK_DEV)
    ]

    odd = lax.rem(me, 2)
    free = pl.ds(pl.multiple_of((1 - odd) * 3 * ROWS, FB), 2 * ROWS)
    shared = pl.ds(pl.multiple_of(odd * 2 * ROWS, FB), 3 * ROWS)

    def store(r, cols, sem):
        here = pl.ds(r * FB, FB)
        return pltpu.make_async_copy(acc_ref.at[here, cols], ham_hbm.at[here, cols], sem.at[r])

    def add_row(which, r):
        place = sum(
            jnp.where(slot_ref[which, first_slot[which] + s] == me * BLK_DEV + r, s + 1, 0) for s in range(CAP)
        )

        @pl.when(place > 0)
        def _():
            start = pl.ds(pl.multiple_of((first_slot[which] + place - 1) * FB, FB), FB)
            for c in range(KB):
                tile_of(acc_ref, r, which, c)[...] += sources[which][start, c * FB : (c + 1) * FB]

    fetch.wait()
    for r in range(BLK_DEV):
        add_row(1, r)
        add_row(2, r)
        store(r, free, early_sem).start()

        @pl.when(jnp.logical_not(across_rows[r]))
        def _():
            store(r, shared, late_sem).start()

    for j in range(1, 4):
        ham_column(j, 2, wei_a, orb_a, tile_a)
    add(0)
    for r in range(BLK_DEV):

        @pl.when(across_rows[r])
        def _():
            store(r, shared, late_sem).start()

    for r in range(BLK_DEV):
        store(r, free, early_sem).wait()
        store(r, shared, late_sem).wait()


def local(devices, density_rows, center_x, center_y, center_z, exponent, brick_blocks):
    params = [x.reshape(-1, 1, FB) for x in (center_x, center_y, center_z, exponent)]
    blocks = brick_blocks.T
    vmem = pl.BlockSpec(memory_space=pltpu.VMEM)
    smem = pl.BlockSpec(memory_space=pltpu.SMEM)
    anywhere = pl.BlockSpec(memory_space=pl.ANY)
    *held, tiles_in, lists = pl.pallas_call(
        functools.partial(main_kernel, devices),
        out_shape=(
            pltpu.VMEM((SIDE, LAYER), f32),
            pltpu.VMEM((KB * FB, CELLS), bf16),
            pltpu.VMEM((NEAR * FB, CELLS), bf16),
            pltpu.VMEM((BOTH * FB, KB * FB), f32),
            pltpu.VMEM((PAIR, PAIR), f32),
            pltpu.VMEM((ROWS + FB, COLS), f32),
            jax.ShapeDtypeStruct((NEAR * FB, KB * FB), f32),
            jax.ShapeDtypeStruct((8, FB), jnp.int32),
        ),
        in_specs=[smem, anywhere] + [vmem] * 4,
        out_specs=(vmem,) * 6 + (anywhere,) * 2,
        scratch_shapes=[
            pltpu.VMEM((BLK_DEV, 5 * BLK_DEV, FB, FB), bf16),
            pltpu.VMEM((KB * FB, CELLS), bf16),
            pltpu.VMEM((NEAR * FB, KB * FB), bf16),
            pltpu.VMEM((BOTH * FB, KB * FB), bf16),
            pltpu.VMEM((NEAR * FB, KB * FB), bf16),
            pltpu.VMEM((NEAR * FB, KB * FB), bf16),
            pltpu.VMEM((BOTH * FB, CELLS), bf16),
            pltpu.VMEM((2, LAYER, FB), f32),
            pltpu.VMEM((3 * SIDE, SIDE * FB), bf16),
            pltpu.VMEM((2, SIDE, LAYER), f32),
            pltpu.VMEM((2, SIDE, LAYER), f32),
            pltpu.VMEM((1, 1, FB), f32),
            pltpu.VMEM((2, SIDE, LAYER), f32),
            pltpu.VMEM((2, 8, LAYER), f32),
            pltpu.VMEM((2, 8, LAYER), f32),
            pltpu.VMEM((devices - 1, 1, FB), f32),
            pltpu.SMEM((8, FB), jnp.int32),
            pltpu.SemaphoreType.DMA,
            pltpu.SemaphoreType.DMA((2,)),
            pltpu.SemaphoreType.DMA((5,)),
            pltpu.SemaphoreType.DMA((5,)),
            pltpu.SemaphoreType.DMA((2,)),
            pltpu.SemaphoreType.DMA((2,)),
            pltpu.SemaphoreType.DMA((2,)),
            pltpu.SemaphoreType.DMA,
        ],
        compiler_params=pltpu.CompilerParams(collective_id=0, has_side_effects=True, vmem_limit_bytes=VMEM_BYTES),
        name="build_tiles",
    )(blocks, density_rows.reshape(BLK_DEV, FB, COLS), *params)
    held = [pltpu.with_memory_space_constraint(x, pltpu.VMEM) for x in held]
    potential, ham, _ = pl.pallas_call(
        functools.partial(out_kernel, devices),
        out_shape=(
            jax.ShapeDtypeStruct((1, CELLS), f32),
            jax.ShapeDtypeStruct((ROWS, COLS), f32),
            pltpu.VMEM((ROWS + FB, COLS), f32),
        ),
        in_specs=[anywhere] + [vmem] * 6 + [anywhere],
        out_specs=(vmem, anywhere, vmem),
        input_output_aliases={6: 2},
        scratch_shapes=[
            pltpu.VMEM((NEAR * FB, KB * FB), f32),
            pltpu.VMEM((NEAR * FB, KB * FB), f32),
            pltpu.SMEM((8, FB), jnp.int32),
            pltpu.SemaphoreType.DMA,
            pltpu.SemaphoreType.DMA,
            pltpu.SemaphoreType.DMA((BLK_DEV,)),
            pltpu.SemaphoreType.DMA((BLK_DEV,)),
        ],
        compiler_params=pltpu.CompilerParams(vmem_limit_bytes=VMEM_BYTES),
        name="place_tiles",
    )(lists, *held, tiles_in)
    return potential, ham


def solution(mesh):
    placed = (P("dev", None), P(), P(), P(), P(), P())
    return jax.shard_map(
        functools.partial(local, mesh.shape["dev"]),
        mesh=mesh,
        in_specs=placed,
        out_specs=(P("dev", None), P("dev", None)),
        check_vma=False,
    )
```

```python
import functools
import math

import jax
import jax.numpy as jnp
from jax import lax
from jax.experimental import pallas as pl
from jax.experimental.pallas import tpu as pltpu
from jax.sharding import PartitionSpec as P

FB = 128
KB = 8
CAP = 4
BLK_DEV = 6
SIDE = 16
LAYER = SIDE * SIDE
CELLS = SIDE * SIDE * SIDE
COLS = 5 * BLK_DEV * FB
ROWS = BLK_DEV * FB
PAIR = 2 * FB
NEAR = 4
BOTH = 6
CHUNK = 4 * LAYER
VMEM_BYTES = 33 * 1024 * 1024

omega = 2.0 / 3.0
four_pi = 4.0 * math.pi
slater = (3.0 / math.pi) ** (1.0 / 3.0)
f32 = jnp.float32
bf16 = jnp.bfloat16


def wrapped(distance):
    moved = distance + 0.5
    return (moved - jnp.floor(moved)) - 0.5


SORT = (
    ((0, 1), (2, 3), (4, 5), (6, 7)),
    ((0, 2), (1, 3), (4, 6), (5, 7)),
    ((1, 2), (5, 6)),
    ((0, 4), (1, 5), (2, 6), (3, 7)),
    ((2, 4), (3, 5)),
    ((1, 2), (3, 4), (5, 6)),
)


def order_blocks(which, brick, first, second, me, devices, bb_ref, slot_ref):
    keys = []
    for j in range(KB):
        block = bb_ref[j, brick]
        owner = lax.div(block, BLK_DEV)
        rank = jnp.where(owner == first, 0, jnp.where(owner == second, 1 << 20, 2 << 20))
        keys.append(rank + (owner * 8 + (block - owner * BLK_DEV)))
    for layer in SORT:
        for i, j in layer:
            keys[i], keys[j] = jnp.minimum(keys[i], keys[j]), jnp.maximum(keys[i], keys[j])
    for s, key in enumerate(keys):
        code = key & ((1 << 20) - 1)
        owner = code >> 3
        local = code & 7
        step = owner - me + 2
        step = jnp.where(step < 0, step + devices, jnp.where(step >= devices, step - devices, step))
        slot_ref[which, s] = owner * BLK_DEV + local
        slot_ref[3 + which, s] = jnp.minimum(step, 4) * BLK_DEV + local


def pair_of(me):
    return me + 1 - 2 * lax.rem(me, 2)


def across_of(me, devices):
    return lax.rem(me + 2 * lax.rem(me, 2) - 1 + devices, devices)


def factors(block, brick, devices, param_refs):
    point = (lax.broadcasted_iota(jnp.int32, (SIDE, FB), 0).astype(f32) + 0.5) / SIDE
    owner = lax.div(block, BLK_DEV)
    offset = (lax.rem(brick - owner + 1 + devices, devices) - 1).astype(f32)
    mid_x, mid_y, mid_z, rate = [ref[block] for ref in param_refs]
    rate = -rate
    along_x = (offset + point) - mid_x
    along_y = wrapped(point - mid_y)
    along_z = wrapped(point - mid_z)
    return jnp.exp(rate * along_x * along_x), jnp.exp(rate * along_y * along_y), jnp.exp(rate * along_z * along_z)


def plane(factor_y, factor_z, rows_ref):
    for j in range(SIDE):
        rows_ref[j * SIDE : (j + 1) * SIDE, :] = factor_y[j : j + 1] * factor_z
    return rows_ref[...].T


def spread_matrix(spread_ref):
    shape = spread_ref.shape
    source = lax.rem(lax.broadcasted_iota(jnp.int32, shape, 0), SIDE)
    target = lax.broadcasted_iota(jnp.int32, shape, 1) // FB
    spread_ref[...] = jnp.where(source == target, 1.0, 0.0).astype(bf16)


def fill_block(which, a, brick, devices, slot_ref, param_refs, rows_ref, spread_ref, orb_ref):
    factor_x, factor_y, factor_z = factors(slot_ref[which, a], brick, devices, param_refs)
    high = factor_x.astype(bf16)
    rest = factor_x - high.astype(f32)
    middle = rest.astype(bf16)
    low = (rest - middle.astype(f32)).astype(bf16)
    parts = jnp.concatenate([high, middle, low], axis=0)
    factor_yz = plane(factor_y, factor_z, rows_ref)
    start = pl.multiple_of(a * FB, FB)
    for n in range(SIDE // 2):
        wide = lax.dot_general(
            parts,
            spread_ref[:, n * PAIR : (n + 1) * PAIR],
            (((0,), (0,)), ((), ())),
            preferred_element_type=f32,
        )
        for h in range(2):
            one = wide[:, h * FB : (h + 1) * FB]
            i = 2 * n + h
            orb_ref[pl.ds(start, FB), i * LAYER : (i + 1) * LAYER] = jnp.concatenate(
                [one * factor_yz[:, :FB], one * factor_yz[:, FB:]], axis=1
            ).astype(bf16)


def fill_lanes(which, a, brick, devices, slot_ref, param_refs, rows_ref, orb_ref):
    factor_x, factor_y, factor_z = factors(slot_ref[which, a], brick, devices, param_refs)
    along = factor_x.T
    factor_yz = plane(factor_y, factor_z, rows_ref)
    start = pl.multiple_of(a * FB, FB)
    for i in range(SIDE):
        orb_ref[pl.ds(start, FB), i * LAYER : (i + 1) * LAYER] = (along[:, i : i + 1] * factor_yz).astype(bf16)


def fold(mat_ref, pairs):
    for i in range(pairs):
        for j in range(i + 1, pairs):
            above = mat_ref[i * PAIR : (i + 1) * PAIR, j * PAIR : (j + 1) * PAIR].astype(f32)
            below = mat_ref[j * PAIR : (j + 1) * PAIR, i * PAIR : (i + 1) * PAIR].astype(f32)
            mat_ref[i * PAIR : (i + 1) * PAIR, j * PAIR : (j + 1) * PAIR] = (above + below.T).astype(bf16)


def density_chunk(j, pairs, mat_ref, orb_ref, pd_ref, t):
    cells = pl.ds(pl.multiple_of(j * CHUNK, CHUNK), CHUNK)
    total = jnp.zeros((1, CHUNK), f32)
    for i in range(pairs):
        applied = jnp.dot(
            mat_ref[i * PAIR : (i + 1) * PAIR, i * PAIR :], orb_ref[i * PAIR :, cells], preferred_element_type=f32
        )
        own = orb_ref[i * PAIR : (i + 1) * PAIR, cells].astype(f32)
        total = total + jnp.sum(own * applied, axis=0, keepdims=True)
    for q in range(CHUNK // LAYER):
        pd_ref[t, pl.ds(j * (CHUNK // LAYER) + q, 1), :] = total[:, q * LAYER : (q + 1) * LAYER]


def weigh_block(k, orb_ref, pot_ref, t, wei_ref):
    rows = pl.ds(pl.multiple_of(k * FB, FB), FB)
    for i in range(SIDE):
        cells = slice(i * LAYER, (i + 1) * LAYER)
        level = pot_ref[t, i : i + 1, :] * (64.0 / CELLS)
        wei_ref[rows, cells] = (orb_ref[rows, cells].astype(f32) * level).astype(bf16)


def ham_tile(rows, j, wei_ref, orb_ref):
    here = slice(j * PAIR, (j + 1) * PAIR)
    return lax.dot_general(wei_ref[rows, :], orb_ref[here, :], (((1,), (1,)), ((), ())), preferred_element_type=f32)


def ham_column(j, pairs, wei_ref, orb_ref, tile_ref):
    rows = slice(0, PAIR * min(j + 1, pairs))
    here = slice(j * PAIR, (j + 1) * PAIR)
    tile = ham_tile(rows, j, wei_ref, orb_ref)
    tile_ref[rows, here] = tile
    if j < pairs:
        for i in range(j):
            tile_ref[here, i * PAIR : (i + 1) * PAIR] = tile[i * PAIR : (i + 1) * PAIR].T


def potential_of(density, before, after, average):
    scale = omega * four_pi / 6.0
    lane = lax.broadcasted_iota(jnp.int32, (SIDE, LAYER), 1) % SIDE
    row = lax.broadcasted_iota(jnp.int32, (SIDE, LAYER), 0)

    def moved(x, steps, axis):
        return pltpu.roll(x, steps % x.shape[axis], axis)

    source = density - average
    one = scale * source
    up = jnp.where(row == 0, scale * (before - average), moved(one, 1, 0))
    down = jnp.where(row == SIDE - 1, scale * (after - average), moved(one, -1, 0))
    beside = up + down + moved(one, SIDE, 1) + moved(one, -SIDE, 1)
    beside = beside + jnp.where(lane == 0, moved(one, 1 - SIDE, 1), moved(one, 1, 1))
    beside = beside + jnp.where(lane == SIDE - 1, moved(one, SIDE - 1, 1), moved(one, -1, 1))
    two = one + omega * ((four_pi * source + beside) / 6.0 - one)
    size = jnp.abs(density)
    safe = jnp.where(size > 0.0, size, 1.0)
    root = jnp.exp(jnp.log(safe) / 3.0)
    root = root - (root - safe / (root * root)) / 3.0
    root = jnp.where(size > 0.0, root, 0.0)
    root = jnp.where(density < 0.0, -root, root)
    return two - slater * root


def main_kernel(
    devices,
    bb_ref,
    rows_hbm,
    cx,
    cy,
    cz,
    ex,
    out_ref,
    orb_a,
    wei_a,
    tile_b,
    corner,
    acc_ref,
    tiles_hbm,
    lists_hbm,
    rows_vmem,
    orb_b,
    mat_a,
    mat_b,
    mat_in,
    mat_out,
    wei_b,
    plane_ref,
    spread_ref,
    pd_ref,
    pot_ref,
    sum_ref,
    full_in,
    before_in,
    after_in,
    sums,
    slot_ref,
    load_sem,
    mat_sem,
    send_sem,
    recv_sem,
    all_sem,
    tile_send,
    tile_recv,
    list_sem,
):
    me = lax.axis_index("dev")
    odd = lax.rem(me, 2)
    pair = pair_of(me)
    across = across_of(me, devices)
    barrier = pltpu.get_barrier_semaphore()

    def at(step):
        return lax.rem(me + step + devices, devices)

    def greet(k, carry):
        pl.semaphore_signal(barrier, inc=1, device_id=(at(k),), device_id_type=pl.DeviceIdType.MESH)
        return carry

    def load(c, carry):
        col = pl.ds(pl.multiple_of(c * FB, FB), FB)
        pltpu.make_async_copy(rows_hbm.at[:, :, col], rows_vmem.at[:, c], load_sem).start()
        return carry

    lax.fori_loop(0, 5 * BLK_DEV, load, 0)
    lax.fori_loop(1, devices, greet, 0)

    lists = ((across, me, me), (me, pair, me), (pair, me, pair))
    for which, (brick, first, second) in enumerate(lists):
        order_blocks(which, brick, first, second, me, devices, bb_ref, slot_ref)

    keep_lists = pltpu.make_async_copy(slot_ref, lists_hbm, list_sem)
    keep_lists.start()
    params = (cx, cy, cz, ex)
    spread_matrix(spread_ref)

    def fill_a(a, carry):
        for h in range(2):
            fill_block(0, 2 * a + h, across, devices, slot_ref, params, plane_ref.at[h], spread_ref, orb_a)
        return carry

    lax.fori_loop(0, KB // 2, fill_a, 0)
    pltpu.make_async_copy(rows_vmem, rows_vmem, load_sem).wait()

    def gather(which, a, target, other=None):
        block = slot_ref[which, a]
        owner = lax.div(block, BLK_DEV)
        mask = jnp.full((FB, PAIR), (owner == me).astype(f32), f32).astype(bf16)
        row = block - owner * BLK_DEV
        here = slice(a * FB, (a + 1) * FB)
        for c in range(0, KB, 2):
            there = slice(c * FB, (c + 2) * FB)
            tiles = [rows_vmem[row, slot_ref[3 + which, c + h]] for h in range(2)]
            tile = jnp.concatenate(tiles, axis=1) * mask
            target[here, there] = tile if other is None else tile + other[here, there]

    for a in range(NEAR):
        gather(2, a, mat_out)
    for a in range(NEAR):
        gather(0, a, mat_a)
    give = pltpu.make_async_remote_copy(
        src_ref=mat_out,
        dst_ref=mat_in,
        send_sem=mat_sem.at[0],
        recv_sem=mat_sem.at[1],
        device_id=(pair,),
        device_id_type=pl.DeviceIdType.MESH,
    )
    fold(mat_a, 2)

    def density_a(j, carry):
        for h in range(2):
            fill_lanes(1, 2 * j + h, me, devices, slot_ref, params, plane_ref.at[h], orb_b)
        density_chunk(j, 2, mat_a, orb_a, pd_ref, odd)
        return carry

    def density_b(j, carry):
        density_chunk(j, 3, mat_b, orb_b, pd_ref, 1 - odd)
        return carry

    lax.fori_loop(0, 1, density_a, 0)
    pl.semaphore_wait(barrier, devices - 1)
    give.start()
    lax.fori_loop(1, CELLS // CHUNK, density_a, 0)
    give.wait()
    mat_b[0:PAIR, :] = mat_in[0:PAIR, :]
    for a in range(2, NEAR):
        gather(1, a, mat_b, mat_in)
    for a in range(NEAR, BOTH):
        gather(1, a, mat_b)
    fold(mat_b, 3)
    lax.fori_loop(0, CELLS // CHUNK, density_b, 0)
    layer = jnp.sum(pd_ref[0] + pd_ref[1], axis=0, keepdims=True)
    sum_ref[0] = layer[:, :FB] + layer[:, FB:]

    def to_all(k):
        return pltpu.make_async_remote_copy(
            src_ref=sum_ref.at[0],
            dst_ref=sums.at[k - 1],
            send_sem=all_sem.at[0],
            recv_sem=all_sem.at[1],
            device_id=(at(k),),
            device_id_type=pl.DeviceIdType.MESH,
        )

    def start_sum(k, carry):
        to_all(k).start()
        return carry

    low = lax.rem(me - 1 + odd + devices, devices)
    plan = (
        (pd_ref, full_in, across, 0),
        (pd_ref.at[1, pl.ds(8, 8)], before_in.at[odd], lax.rem(low + 2, devices), 1 + odd),
        (pd_ref.at[1, pl.ds(8, 8)], before_in.at[odd], lax.rem(low + 3, devices), 1 + odd),
        (pd_ref.at[0, pl.ds(0, 8)], after_in.at[odd], lax.rem(low - 2 + devices, devices), 3 + odd),
        (pd_ref.at[0, pl.ds(0, 8)], after_in.at[odd], lax.rem(low - 1 + devices, devices), 3 + odd),
    )
    copies = [
        pltpu.make_async_remote_copy(
            src_ref=src,
            dst_ref=dst,
            send_sem=send_sem.at[q],
            recv_sem=recv_sem.at[r],
            device_id=(device,),
            device_id_type=pl.DeviceIdType.MESH,
        )
        for q, (src, dst, device, r) in enumerate(plan)
    ]
    lax.fori_loop(1, devices, start_sum, 0)
    for copy in copies:
        copy.start()
    acc_ref[...] = jnp.zeros(acc_ref.shape, f32)
    pltpu.make_async_copy(full_in, full_in, recv_sem.at[0]).wait()
    for s in range(2):
        pltpu.make_async_copy(before_in.at[s], before_in.at[s], recv_sem.at[1 + s]).wait()
        pltpu.make_async_copy(after_in.at[s], after_in.at[s], recv_sem.at[3 + s]).wait()
    pltpu.make_async_copy(sums, sums, all_sem.at[1]).wait()

    total = jnp.sum(sums[...], axis=0) + sum_ref[0]
    average = jnp.sum(total, axis=1, keepdims=True) / (devices * CELLS)
    first = pd_ref[0] + full_in[0]
    second = pd_ref[1] + full_in[1]
    behind = (before_in[0] + before_in[1])[7:]
    ahead = (after_in[0] + after_in[1])[:1]
    pot_ref[0] = potential_of(first, behind, second[:1], average)
    pot_ref[1] = potential_of(second, first[SIDE - 1 :], ahead, average)
    out_ref[...] = pot_ref[1 - odd]

    def weigh_a(k, carry):
        weigh_block(k, orb_a, pot_ref, odd, wei_a)
        return carry

    def weigh_b(k, carry):
        weigh_block(k, orb_b, pot_ref, 1 - odd, wei_b)
        return carry

    lax.fori_loop(0, NEAR, weigh_b, 0)

    def give_tiles(n, cells):
        return pltpu.make_async_remote_copy(
            src_ref=tile_b.at[pl.ds(0, NEAR * FB), cells],
            dst_ref=tiles_hbm.at[:, cells],
            send_sem=tile_send.at[n],
            recv_sem=tile_recv.at[n],
            device_id=(pair,),
            device_id_type=pl.DeviceIdType.MESH,
        )

    gives = [give_tiles(n, pl.ds(n * 2 * PAIR, 2 * PAIR)) for n in range(2)]
    for j in (3, 2):
        ham_column(j, 2, wei_b, orb_b, tile_b)
        weigh_b(NEAR + 3 - j, 0)
        weigh_a(3 - j, 0)
    gives[1].start()
    for j in (1, 0):
        ham_column(j, 2, wei_b, orb_b, tile_b)
        weigh_a(3 - j, 0)
    gives[0].start()
    last = slice(2 * PAIR, 3 * PAIR)
    for j in (2, 3):
        tile_b[last, j * PAIR : (j + 1) * PAIR] = ham_tile(last, j, wei_b, orb_b)
    for i in range(2):
        tile_b[last, i * PAIR : (i + 1) * PAIR] = tile_b[i * PAIR : (i + 1) * PAIR, last].T
    corner[...] = ham_tile(slice(0, PAIR), 0, wei_a, orb_a)
    for copy in copies:
        copy.wait_send()
    pltpu.make_async_copy(sums, sums, all_sem.at[0]).wait()
    for copy in gives:
        copy.wait()
    keep_lists.wait()


def out_kernel(
    devices,
    lists_hbm,
    pot_in,
    orb_a,
    wei_a,
    tile_b,
    corner,
    acc_in,
    tiles_hbm,
    pot_out,
    ham_hbm,
    acc_ref,
    tile_a,
    tile_in,
    slot_ref,
    in_sem,
    list_sem,
    early_sem,
    late_sem,
    last_sem,
):
    me = lax.axis_index("dev")
    lay = pltpu.make_async_copy(lists_hbm, slot_ref, list_sem)
    lay.start()
    fetch = pltpu.make_async_copy(tiles_hbm, tile_in, in_sem)
    fetch.start()
    for i in range(SIDE):
        pot_out[:, i * LAYER : (i + 1) * LAYER] = pot_in[i : i + 1, :]
    tile_a[0:PAIR, 0:PAIR] = corner[...]
    lay.wait()
    sources = (tile_a, tile_b, tile_in)
    first_slot = (0, 2, 0)

    def owned(which, s):
        block = slot_ref[which, first_slot[which] + s]
        owner = lax.div(block, BLK_DEV)
        return owner == me, block - owner * BLK_DEV

    def tile_of(ref, row, which, c):
        col = pl.multiple_of(slot_ref[3 + which, c] * FB, FB)
        return ref.at[pl.ds(pl.multiple_of(row * FB, FB), FB), pl.ds(col, FB)]

    def add_slot(which, s):
        mine, row = owned(which, s)
        row = jnp.where(mine, row, BLK_DEV)
        start = (first_slot[which] + s) * FB
        for c in range(KB):
            tile_of(acc_ref, row, which, c)[...] += sources[which][start : start + FB, c * FB : (c + 1) * FB]

    def add(which):
        for s in range(CAP):
            add_slot(which, s)

    across_rows = [
        sum((slot_ref[0, s] == me * BLK_DEV + r).astype(jnp.int32) for s in range(CAP)) > 0 for r in range(BLK_DEV)
    ]

    odd = lax.rem(me, 2)
    free = pl.ds(pl.multiple_of((1 - odd) * 3 * ROWS, FB), 2 * ROWS)
    shared = pl.ds(pl.multiple_of(odd * 2 * ROWS, FB), 3 * ROWS)

    def store(r, cols, sem):
        here = pl.ds(r * FB, FB)
        return pltpu.make_async_copy(acc_ref.at[here, cols], ham_hbm.at[here, cols], sem.at[r])

    add(1)
    fetch.wait()
    add(2)
    for r in range(BLK_DEV):
        store(r, free, early_sem).start()

        @pl.when(jnp.logical_not(across_rows[r]))
        def _():
            store(r, shared, late_sem).start()

    for j in range(1, 4):
        ham_column(j, 2, wei_a, orb_a, tile_a)
    def store_slot(s, act):
        mine, row = owned(0, s)

        @pl.when(mine)
        def _():
            here = pl.ds(pl.multiple_of(row * FB, FB), FB)
            act(pltpu.make_async_copy(acc_ref.at[here, shared], ham_hbm.at[here, shared], last_sem.at[s]))

    for s in range(CAP):
        add_slot(0, s)
        store_slot(s, lambda copy: copy.start())
    for r in range(BLK_DEV):
        store(r, free, early_sem).wait()

        @pl.when(jnp.logical_not(across_rows[r]))
        def _():
            store(r, shared, late_sem).wait()

    for s in range(CAP):
        store_slot(s, lambda copy: copy.wait())


def local(devices, density_rows, center_x, center_y, center_z, exponent, brick_blocks):
    params = [x.reshape(-1, 1, FB) for x in (center_x, center_y, center_z, exponent)]
    blocks = brick_blocks.T
    vmem = pl.BlockSpec(memory_space=pltpu.VMEM)
    smem = pl.BlockSpec(memory_space=pltpu.SMEM)
    anywhere = pl.BlockSpec(memory_space=pl.ANY)
    *held, tiles_in, lists = pl.pallas_call(
        functools.partial(main_kernel, devices),
        out_shape=(
            pltpu.VMEM((SIDE, LAYER), f32),
            pltpu.VMEM((KB * FB, CELLS), bf16),
            pltpu.VMEM((NEAR * FB, CELLS), bf16),
            pltpu.VMEM((BOTH * FB, KB * FB), f32),
            pltpu.VMEM((PAIR, PAIR), f32),
            pltpu.VMEM((ROWS + FB, COLS), f32),
            jax.ShapeDtypeStruct((NEAR * FB, KB * FB), f32),
            jax.ShapeDtypeStruct((8, FB), jnp.int32),
        ),
        in_specs=[smem, anywhere] + [vmem] * 4,
        out_specs=(vmem,) * 6 + (anywhere,) * 2,
        scratch_shapes=[
            pltpu.VMEM((BLK_DEV, 5 * BLK_DEV, FB, FB), bf16),
            pltpu.VMEM((KB * FB, CELLS), bf16),
            pltpu.VMEM((NEAR * FB, KB * FB), bf16),
            pltpu.VMEM((BOTH * FB, KB * FB), bf16),
            pltpu.VMEM((NEAR * FB, KB * FB), bf16),
            pltpu.VMEM((NEAR * FB, KB * FB), bf16),
            pltpu.VMEM((BOTH * FB, CELLS), bf16),
            pltpu.VMEM((2, LAYER, FB), f32),
            pltpu.VMEM((3 * SIDE, SIDE * FB), bf16),
            pltpu.VMEM((2, SIDE, LAYER), f32),
            pltpu.VMEM((2, SIDE, LAYER), f32),
            pltpu.VMEM((1, 1, FB), f32),
            pltpu.VMEM((2, SIDE, LAYER), f32),
            pltpu.VMEM((2, 8, LAYER), f32),
            pltpu.VMEM((2, 8, LAYER), f32),
            pltpu.VMEM((devices - 1, 1, FB), f32),
            pltpu.SMEM((8, FB), jnp.int32),
            pltpu.SemaphoreType.DMA,
            pltpu.SemaphoreType.DMA((2,)),
            pltpu.SemaphoreType.DMA((5,)),
            pltpu.SemaphoreType.DMA((5,)),
            pltpu.SemaphoreType.DMA((2,)),
            pltpu.SemaphoreType.DMA((2,)),
            pltpu.SemaphoreType.DMA((2,)),
            pltpu.SemaphoreType.DMA,
        ],
        compiler_params=pltpu.CompilerParams(collective_id=0, has_side_effects=True, vmem_limit_bytes=VMEM_BYTES),
        name="build_tiles",
    )(blocks, density_rows.reshape(BLK_DEV, FB, COLS), *params)
    held = [pltpu.with_memory_space_constraint(x, pltpu.VMEM) for x in held]
    potential, ham, _ = pl.pallas_call(
        functools.partial(out_kernel, devices),
        out_shape=(
            jax.ShapeDtypeStruct((1, CELLS), f32),
            jax.ShapeDtypeStruct((ROWS, COLS), f32),
            pltpu.VMEM((ROWS + FB, COLS), f32),
        ),
        in_specs=[anywhere] + [vmem] * 6 + [anywhere],
        out_specs=(vmem, anywhere, vmem),
        input_output_aliases={6: 2},
        scratch_shapes=[
            pltpu.VMEM((NEAR * FB, KB * FB), f32),
            pltpu.VMEM((NEAR * FB, KB * FB), f32),
            pltpu.SMEM((8, FB), jnp.int32),
            pltpu.SemaphoreType.DMA,
            pltpu.SemaphoreType.DMA,
            pltpu.SemaphoreType.DMA((BLK_DEV,)),
            pltpu.SemaphoreType.DMA((BLK_DEV,)),
            pltpu.SemaphoreType.DMA((CAP,)),
        ],
        compiler_params=pltpu.CompilerParams(vmem_limit_bytes=VMEM_BYTES),
        name="place_tiles",
    )(lists, *held, tiles_in)
    return potential, ham


def solution(mesh):
    placed = (P("dev", None), P(), P(), P(), P(), P())
    return jax.shard_map(
        functools.partial(local, mesh.shape["dev"]),
        mesh=mesh,
        in_specs=placed,
        out_specs=(P("dev", None), P("dev", None)),
        check_vma=False,
    )
```
